256 devices in a mesh: mem: 16 (over z, core), dom: 16 (over x, y).
Axes of the slice: x: 4, y: 4, z: 8, core: 2. Of those that a mesh axis runs over, the one named last changes fastest.
Arguments:
- prior_sample_set: float32 [256, 32, 64, 128], P('mem', None, 'dom'), may hold values from -6 to 6
- crossing_number_north: float32 [32], replicated, may hold values from -0.7 to 0.7
- crossing_number_east: float32 [32], replicated, may hold values from -0.7 to 0.7
- spreading_number: float32 [32], replicated, may hold values from 0.01 to 0.08
- obs_cell: int32 [16384], P('dom'), may hold values from 0 to 16383
- obs_value: float32 [16384], P('dom'), may hold values from -6 to 6
- obs_var: float32 [16384], P('dom'), may hold values from 0.25 to 4
- tile_list: int32 [16, 32, 256], P('dom', 'mem'), may hold values from 0 to 3071, as said below
- tile_count: int32 [16, 32], P('dom', 'mem'), may hold values from 1 to 256, as said below
Outputs:
- analysis: float32 [256, 32, 64, 128], P('mem', None, 'dom')
The draws below stay inside these ranges and needn't reach their ends.
Inputs may be any that keep to these rules, and one draw needn't show every extreme that they name: `tile_list`: entries of one tile are distinct; entry p names observation p mod 1024 of the strip before the tile's own, its own, or the one after, periodically, as p // 1024 is 0, 1 or 2. Only the first tile_count entries are used. `tile_count`: some tile uses 256 observations in every draw. `obs_cell`: numbered by level, then row of the strip, then column.
All inputs are finite; a program needn't handle non-finite values.
Results may differ from the reference program's by a relative error of at most 0.0003.
Values sent between devices are 32-bit elements; how exact they have to be, the bound alone decides.
No kernel may reach another device: no remote copies, remote signals or barrier semaphores. Data moves between devices by JAX's collectives and lax.ppermute only.
A program may use at most 64 MiB of HBM per device.

```python
import math
import jax
import jax.numpy as jnp
from jax import lax

MEMBERS = 256
LAYER_COUNT = 32
CX = 4
MESH_WIDTH = 128
MESH_HEIGHT = 64
PATCH_EXTENT = 4
TILES_X = 16
TILES_Y = 32
NOBS = 1024
OBS = 16384
CAP = 256
LOC = 8
STEPS = 3
NS_ITERS = 5
N_DOM = 16


def pick_entries(one_key):
    return jax.random.permutation(one_key, 3 * NOBS)[:CAP]


def draw_tile_list(key, part):
    tile_keys = jax.random.split(key, TILES_X * TILES_Y)
    picked = jax.vmap(pick_entries)(tile_keys)
    return picked.reshape(TILES_X, TILES_Y, CAP).astype(jnp.int32)


def draw_tile_count(key, part):
    left_key, right_key, third_key = jax.random.split(key, 3)
    tile_shape = (TILES_X, TILES_Y)
    left_factor = jax.random.randint(left_key, tile_shape, 0, CAP)
    right_factor = jax.random.randint(right_key, tile_shape, 0, CAP)
    counts = 1 + left_factor * right_factor // CAP
    busiest = jax.random.randint(third_key, (), 0, TILES_X * TILES_Y)
    raveled_offset = jnp.arange(TILES_X * TILES_Y).reshape(tile_shape)
    return jnp.where(raveled_offset == busiest, CAP, counts).astype(jnp.int32)


def place_ends(result, stream_key, low, high):
    index_at = [jax.random.randint(jax.random.fold_in(stream_key, axis), (), 0, length) for axis, length in enumerate(result.shape)]
    widest = result.shape.index(max(result.shape))
    beside = index_at[:widest] + [(index_at[widest] + 1) % result.shape[widest]] + index_at[widest + 1:]
    return result.at[tuple(index_at)].set(low).at[tuple(beside)].set(high)


def block_levels(key, dims, pieces, least, high):
    def one(dim, blocks):
        draws = jax.random.uniform(jax.random.fold_in(jax.random.fold_in(key, 6), dim), (blocks,), jnp.float32, least / len(pieces), high / len(pieces))
        return jnp.repeat(jnp.exp(draws), dims[dim] // blocks).reshape((-1,) + (1,) * (len(dims) - dim - 1))

    level = one(*pieces[0])
    for cut in pieces[1:]:
        level = level * one(*cut)
    return level


def bell_draw(key, dims, scale, limit, pieces=(), held_as=jnp.bfloat16):
    entries = jax.random.normal(key, dims, jnp.float32) * scale
    if len(pieces) > 0:
        entries = block_levels(key, dims, pieces, -0.22, 0.18) * entries
    return jnp.clip(entries, min=-limit, max=limit).astype(held_as)


def setup_inputs(seed: int = 0) -> dict:
    arg_keys = jax.random.split(jax.random.key(seed), 10)
    prior_sample_set = bell_draw(arg_keys[0], (MEMBERS, LAYER_COUNT, MESH_HEIGHT, MESH_WIDTH), 1.0, 6.0, ((0, 16), (2, 16)), jnp.float32)
    crossing_number_north = jnp.clip(jax.random.uniform(arg_keys[1], (LAYER_COUNT,), jnp.float32, -0.7, 0.7), -0.7, 0.7)
    crossing_number_east = jnp.clip(jax.random.uniform(arg_keys[2], (LAYER_COUNT,), jnp.float32, -0.7, 0.7), -0.7, 0.7)
    spreading_number = jnp.clip(jnp.exp(jax.random.uniform(arg_keys[3], (LAYER_COUNT,), jnp.float32, math.log(0.01), math.log(0.08))), 0.01, 0.08)
    obs_cell = place_ends(jax.random.randint(arg_keys[4], (OBS,), 0, LAYER_COUNT * CX * MESH_WIDTH), jax.random.fold_in(arg_keys[4], 1), 0, (LAYER_COUNT * CX * MESH_WIDTH) - 1).astype(jnp.int32)
    obs_value = bell_draw(arg_keys[5], (OBS,), 1.0, 6.0, ((0, 16),), jnp.float32)
    obs_var = jnp.clip(jnp.exp(math.log(4.0) - 2.7725887 * jax.random.uniform(arg_keys[6], (OBS,), jnp.float32) ** block_levels(arg_keys[6], (OBS,), ((0, 16),), -0.2, 0.2)), 0.25, 4.0)
    tile_list = draw_tile_list(jax.random.fold_in(arg_keys[9], 71), 0)
    tile_count = draw_tile_count(jax.random.fold_in(arg_keys[9], 71), 0)
    return dict(prior_sample_set=prior_sample_set, crossing_number_north=crossing_number_north, crossing_number_east=crossing_number_east, spreading_number=spreading_number, obs_cell=obs_cell, obs_value=obs_value, obs_var=obs_var, tile_list=tile_list, tile_count=tile_count)


inflation = 1.1
highest = lax.Precision.HIGHEST

def tendency(field_in, speed_x, speed_y, mixing):
    east_side = jnp.roll(field_in, -1, 1)
    west_side = jnp.roll(field_in, 1, 1)
    north_side = jnp.roll(field_in, -1, 2)
    south_side = jnp.roll(field_in, 1, 2)
    return -speed_x[:, None, None] * (east_side - west_side) * 0.5 - speed_y[:, None, None] * (north_side - south_side) * 0.5 + mixing[:, None, None] * (east_side + west_side + north_side + south_side - 4.0 * field_in)

def ensemble_weights(obs_rows, values, variances, place_x, place_y, counts, centre_x, centre_y, width_x, width_y):
    sample_count = obs_rows.shape[0]
    capacity = obs_rows.shape[2]
    ens_mean = lax.optimization_barrier(jnp.mean(obs_rows, axis=0))
    anomaly = obs_rows - ens_mean
    innovation = values - ens_mean
    delta_x = jnp.mod(place_x - centre_x[:, None] + 0.5 * width_x, width_x) - 0.5 * width_x
    delta_y = jnp.mod(place_y - centre_y[:, None] + 0.5 * width_y, width_y) - 0.5 * width_y
    live_slot = jnp.arange(capacity, dtype=jnp.int32)[None, :] < counts[:, None]
    spread = 1.0 + (delta_x * delta_x + delta_y * delta_y) / float(LOC * LOC)
    precision_obs = jnp.where(live_slot, 1.0 / (variances * spread), 0.0)
    weighted = anomaly * precision_obs[None]
    gram_matrix = jnp.einsum('mbc,nbc->bmn', weighted, anomaly, precision=highest)
    identity = jnp.eye(sample_count, dtype=jnp.float32)
    gram_matrix = gram_matrix + (sample_count - 1) / inflation * identity
    norm_scale = jnp.sqrt(lax.optimization_barrier(jnp.sum(gram_matrix * gram_matrix, axis=(1, 2))))
    iterate = gram_matrix / norm_scale[:, None, None]
    root_inverse = jnp.broadcast_to(identity, gram_matrix.shape)
    for repeat in range(NS_ITERS):
        factor = 1.5 * identity - 0.5 * jnp.matmul(root_inverse, iterate, precision=highest)
        iterate = jnp.matmul(iterate, factor, precision=highest)
        root_inverse = jnp.matmul(factor, root_inverse, precision=highest)
    drive_term = jnp.einsum('mbc,bc->bm', weighted, innovation, precision=highest)
    inner_term = jnp.einsum('bij,bj->bi', root_inverse, drive_term, precision=highest)
    mean_shift = jnp.einsum('bij,bj->bi', root_inverse, inner_term, precision=highest) / norm_scale[:, None]
    return jnp.sqrt((sample_count - 1) / norm_scale)[:, None, None] * root_inverse + mean_shift[:, :, None]

def reference(prior_sample_set, crossing_number_north, crossing_number_east, spreading_number, obs_cell, obs_value, obs_var, tile_list, tile_count):

    def one_sample_vector(member_field):
        for repeat in range(STEPS):
            first_section = member_field + tendency(member_field, crossing_number_north, crossing_number_east, spreading_number) / 3.0
            second_section = member_field + tendency(first_section, crossing_number_north, crossing_number_east, spreading_number) * 0.5
            member_field = member_field + tendency(second_section, crossing_number_north, crossing_number_east, spreading_number)
        return member_field
    propagator_operator = lax.map(one_sample_vector, prior_sample_set)
    sample_count = propagator_operator.shape[0]
    strip_index = jnp.arange(N_DOM * NOBS, dtype=jnp.int32) // NOBS
    level_index = obs_cell // (CX * MESH_WIDTH)
    global_row = strip_index * CX + obs_cell // MESH_WIDTH % CX
    col_index = obs_cell % MESH_WIDTH
    raveled_offset = ((level_index * MESH_HEIGHT + global_row) * MESH_WIDTH + col_index).astype(jnp.int32)
    measured_samples = jnp.take(propagator_operator.reshape(sample_count, LAYER_COUNT * MESH_HEIGHT * MESH_WIDTH), raveled_offset, axis=1)
    pos_x = global_row.astype(jnp.float32)
    pos_y = col_index.astype(jnp.float32)
    per_strip = CX // PATCH_EXTENT

    def tile_row(patch_vertical_offset):
        row_lists = tile_list[patch_vertical_offset]
        strip_here = patch_vertical_offset // per_strip
        source_strip = (strip_here - 1 + row_lists // NOBS) % N_DOM
        index_obs = (source_strip * NOBS + row_lists % NOBS).astype(jnp.int32)
        obs_rows = jnp.take(measured_samples, index_obs, axis=1)
        centre_x = jnp.zeros((TILES_Y,), jnp.float32) + (patch_vertical_offset * PATCH_EXTENT).astype(jnp.float32) + 0.5 * (PATCH_EXTENT - 1)
        centre_y = jnp.arange(TILES_Y, dtype=jnp.int32).astype(jnp.float32) * PATCH_EXTENT + 0.5 * (PATCH_EXTENT - 1)
        weights = ensemble_weights(obs_rows, obs_value[index_obs], obs_var[index_obs], pos_x[index_obs], pos_y[index_obs], tile_count[patch_vertical_offset], centre_x, centre_y, float(MESH_HEIGHT), float(MESH_WIDTH))
        patch_subarray = lax.dynamic_slice_in_dim(propagator_operator, (patch_vertical_offset * PATCH_EXTENT).astype(jnp.int32), PATCH_EXTENT, 2)
        patch_subarray = patch_subarray.reshape(sample_count, LAYER_COUNT, PATCH_EXTENT, TILES_Y, PATCH_EXTENT)
        block_mean = lax.optimization_barrier(jnp.mean(patch_subarray, axis=0))
        update = jnp.einsum('ckm,klicj->mlicj', weights, patch_subarray - block_mean, precision=highest)
        return (block_mean + update).reshape(sample_count, LAYER_COUNT, PATCH_EXTENT, MESH_WIDTH)
    rows_out = lax.map(tile_row, jnp.arange(TILES_X, dtype=jnp.int32))
    return jnp.transpose(rows_out, (1, 2, 0, 3, 4)).reshape(sample_count, LAYER_COUNT, MESH_HEIGHT, MESH_WIDTH)
```

```python
import jax
import jax.numpy as jnp
from jax import lax
from jax.experimental import pallas as pl
from jax.experimental.pallas import tpu as pltpu
from jax.sharding import PartitionSpec as P

LOC = 8
STEPS = 3
NS_ITERS = 5
INFLATION = 1.1

F32 = jnp.float32
BF16 = jnp.bfloat16
LEVELS = 32
ROWS = 4
COLS = 128
CELL_ROWS = LEVELS * ROWS
OBS_CHUNKS = 8
META = 3 * OBS_CHUNKS
PACK = CELL_ROWS + META
SLOT_ROWS = 4
COLS_HERE = 8
SEND = COLS_HERE + SLOT_ROWS
PER_MEM = 16
STRIPS = 16
HEIGHT = STRIPS * ROWS


def lane_gather(values, lanes):
    return jnp.take_along_axis(values, lanes, axis=1, mode="promise_in_bounds")


def forecast_kernel(where_ref, north_ref, east_ref, mix_ref, in_ref, out_ref, meta_ref, q_ref, t1_ref, t2_ref, hx_ref):
    def load(s, _):
        for r in range(ROWS):
            q_ref[pl.ds(s * CELL_ROWS + r * LEVELS, LEVELS), :] = in_ref[
                pl.ds(s * PACK + r, LEVELS, stride=ROWS), :
            ]
        return 0

    lax.fori_loop(0, STRIPS, load, 0)

    def level_group(g, _):
        sub = lax.broadcasted_iota(jnp.int32, (8, COLS), 0)

        def spread(ref):
            value = jnp.full((8, COLS), ref[g * 8], F32)
            for i in range(1, 8):
                value = jnp.where(sub == i, ref[g * 8 + i], value)
            return value

        north, east, mix = spread(north_ref), spread(east_ref), spread(mix_ref)
        up, down = mix - 0.5 * north, mix + 0.5 * north
        right, left = mix - 0.5 * east, mix + 0.5 * east
        mid = -4.0 * mix

        def stage(src, dst, scale):
            a, b, c, d, e = up * scale, down * scale, right * scale, left * scale, mid * scale

            def at(ref, x):
                return ref.at[pl.ds(pl.multiple_of(x * LEVELS + g * 8, 8), 8), :]

            def row(x, carry):
                prev, cur = carry
                nxt = at(src, lax.rem(x + 1, HEIGHT))[...]
                at(dst, x)[...] = (
                    at(q_ref, x)[...]
                    + (a * nxt + b * prev)
                    + (c * pltpu.roll(cur, COLS - 1, 1) + d * pltpu.roll(cur, 1, 1))
                    + e * cur
                )
                return cur, nxt

            lax.fori_loop(0, HEIGHT, row, (at(src, HEIGHT - 1)[...], at(src, 0)[...]), unroll=8)

        def step(_, c):
            stage(q_ref, t1_ref, 1.0 / 3.0)
            stage(t1_ref, t2_ref, 0.5)
            stage(t2_ref, q_ref, 1.0)
            return c

        lax.fori_loop(0, STEPS, step, 0)
        return 0

    lax.fori_loop(0, LEVELS // 8, level_group, 0)

    for g in range(2):
        lanes, rows = [], []
        for j in range(OBS_CHUNKS):
            cell = in_ref[pl.ds(g * 8 * PACK + CELL_ROWS + j, 8, stride=PACK), :].astype(jnp.int32)
            lanes.append(cell & (COLS - 1))
            line = cell >> 7
            rows.append((line & (ROWS - 1)) * LEVELS + (line >> 2))

        def pick(p, acc):
            src = q_ref[pl.ds(p + g * 8 * CELL_ROWS, 8, stride=CELL_ROWS), :]
            return tuple(
                jnp.where(rows[j] == p, lane_gather(src, lanes[j]), acc[j]) for j in range(OBS_CHUNKS)
            )

        acc = lax.fori_loop(
            0, CELL_ROWS, pick, tuple(jnp.zeros((8, COLS), F32) for _ in range(OBS_CHUNKS)), unroll=4
        )
        for j in range(OBS_CHUNKS):
            hx_ref[pl.ds(g * 64 + j, 8, stride=OBS_CHUNKS), :] = acc[j]

    def store(s, _):
        base = pl.multiple_of(s * CELL_ROWS, 8)
        to = pl.multiple_of(s * PACK, 8)
        out_ref[pl.ds(to, CELL_ROWS), :] = q_ref[pl.ds(base, CELL_ROWS), :].T
        for t in range(3):
            strip = lax.rem(s + STRIPS - 1 + t, STRIPS)
            out_ref[pl.ds(to + CELL_ROWS + 8 * t, 8), :] = hx_ref[pl.ds(pl.multiple_of(strip * 8, 8), 8), :]
        return 0

    lax.fori_loop(0, STRIPS, store, 0)

    meta_ref[...] = jnp.zeros_like(meta_ref)
    for t in range(3):
        strip = lax.rem(where_ref[0] + STRIPS - 1 + t, STRIPS)
        for which in range(3):
            meta_ref[pl.ds(t * 64 + which, 8, stride=8), :] = in_ref[
                pl.ds(pl.multiple_of(strip * PACK + CELL_ROWS + which * 8, 8), 8), :
            ]


def select_kernel(where_ref, list_ref, in_ref, out_ref, d_ref):
    for j in range(META):
        d_ref[pl.ds(j * PER_MEM, PER_MEM), :] = in_ref[pl.ds(CELL_ROWS + j, PER_MEM, stride=PACK), :]

    def peer(kb, _):
        to = pl.multiple_of(kb * SEND * PER_MEM, 8)
        for c in range(COLS_HERE):
            out_ref[pl.ds(to + c * PER_MEM, PER_MEM), :] = in_ref[
                pl.ds(kb * COLS_HERE + c, PER_MEM, stride=PACK), :
            ]
        first = lax.bitwise_xor(where_ref[1], kb) * SLOT_ROWS
        for q in range(SLOT_ROWS):
            slot = jnp.broadcast_to(list_ref[pl.ds(first + q, 1), :], (8, COLS))
            lanes = slot & (COLS - 1)
            chunk = slot >> 7
            low = jnp.zeros((8, COLS), F32)
            high = jnp.zeros((8, COLS), F32)
            for j in range(META):
                here = chunk == j
                low = jnp.where(here, lane_gather(d_ref[pl.ds(j * PER_MEM, 8), :], lanes), low)
                high = jnp.where(here, lane_gather(d_ref[pl.ds(j * PER_MEM + 8, 8), :], lanes), high)
            at = to + (COLS_HERE + q) * PER_MEM
            out_ref[pl.ds(at, 8), :] = low
            out_ref[pl.ds(at + 8, 8), :] = high
        return 0

    lax.fori_loop(0, PER_MEM, peer, 0)


def parts(x):
    high = x.astype(BF16)
    return high, (x - high.astype(F32)).astype(BF16)


def product(a, b, dims=(((1,), (0,)), ((), ()))):
    def dot(x, y):
        return lax.dot_general(x, y, dims, preferred_element_type=F32)

    return dot(a[0], b[0]) + (dot(a[0], b[1]) + dot(a[1], b[0]))


def update_kernel(where_ref, count_ref, list_ref, meta_ref, in_ref, out_ref, it_ref, root_ref):
    members = 256
    row_id = lax.broadcasted_iota(jnp.int32, (members, members), 0)
    col_id = lax.broadcasted_iota(jnp.int32, (members, members), 1)
    diagonal = row_id == col_id
    slot_id = lax.broadcasted_iota(jnp.int32, (1, COLS), 1)

    def plus_identity(x, scale):
        return jnp.where(diagonal, x + scale, x)

    norms, drives = [], []
    for t in range(2):
        values, rhos, anomalies = [], [], []
        for h in range(2):
            slot = list_ref[pl.ds(2 * t + h, 1), :]
            wide = jnp.broadcast_to(slot, (8, COLS))
            lanes = wide & (COLS - 1)
            chunk = wide >> 7
            found = jnp.zeros((8, COLS), F32)
            for j in range(META):
                found = jnp.where(chunk == j, lane_gather(meta_ref[pl.ds(j * 8, 8), :], lanes), found)
            line = found[0:1].astype(jnp.int32)
            strip = where_ref[0] + STRIPS - 1 + (slot >> 10)
            strip = strip & (STRIPS - 1)
            place_x = (strip * ROWS + ((line >> 7) & (ROWS - 1))).astype(F32)
            place_y = (line & (COLS - 1)).astype(F32)
            centre_x = (where_ref[0] * 4).astype(F32) + 1.5
            centre_y = ((where_ref[1] * 2 + t) * 4).astype(F32) + 1.5
            dx = place_x - centre_x + 0.5 * HEIGHT
            dx = jnp.where(dx >= HEIGHT, dx - HEIGHT, dx)
            dx = jnp.where(dx < 0, dx + HEIGHT, dx) - 0.5 * HEIGHT
            dy = place_y - centre_y + 0.5 * COLS
            dy = jnp.where(dy >= COLS, dy - COLS, dy)
            dy = jnp.where(dy < 0, dy + COLS, dy) - 0.5 * COLS
            live = slot_id + h * COLS < count_ref[0, t]
            spread = found[2:3] * (1.0 + (dx * dx + dy * dy) / float(LOC * LOC))
            rho = jnp.where(live, 1.0 / spread, 0.0)
            obs = in_ref[:, COLS_HERE + 2 * t + h].reshape(members, COLS)
            mean = jnp.sum(obs, axis=0, keepdims=True) * (1.0 / members)
            values.append(found[1:2] - mean)
            rhos.append(rho)
            anomalies.append(obs - mean)
        anomaly = jnp.concatenate(anomalies, axis=1)
        rho = jnp.concatenate(rhos, axis=1)
        innovation = jnp.concatenate(values, axis=1)
        drives.append(jnp.sum(anomaly * (rho * innovation), axis=1, keepdims=True))
        scaled = parts(anomaly * jnp.sqrt(rho))
        gram = product(scaled, scaled, (((1,), (1,)), ((), ())))
        gram = plus_identity(gram, (members - 1) / INFLATION)
        norm = jnp.sqrt(jnp.sum(jnp.sum(gram * gram, axis=1, keepdims=True), axis=0, keepdims=True))
        norms.append(norm)
        it = gram / norm
        factor = plus_identity(-0.5 * it, 1.5)
        root_ref[t] = factor
        it_ref[t] = product(parts(it), parts(factor))

    def iteration(_, c):
        for t in range(2):
            root, it = parts(root_ref[t]), parts(it_ref[t])
            factor = parts(plus_identity(-0.5 * product(root, it), 1.5))
            it_ref[t] = product(it, factor)
            root_ref[t] = product(factor, root)
        return c

    lax.fori_loop(0, NS_ITERS - 2, iteration, 0)

    for t in range(2):
        root, it = parts(root_ref[t]), parts(it_ref[t])
        factor = parts(plus_identity(-0.5 * product(root, it), 1.5))
        full = product(factor, root)
        inner = jnp.sum(full * drives[t], axis=0, keepdims=True)
        shift = jnp.sum(full * inner, axis=1, keepdims=True) / norms[t]
        scale = jnp.sqrt((members - 1) / norms[t])
        root = parts(full * scale)
        for c in range(4 * t, 4 * t + 4):
            x = in_ref[:, c].reshape(members, COLS)
            mean = jnp.sum(x, axis=0, keepdims=True) * (1.0 / members)
            x = x - mean
            moved = mean + jnp.sum(x * shift, axis=0, keepdims=True)
            out = product(root, parts(x)) + moved
            out_ref[:, c] = out.reshape(PER_MEM, PER_MEM, COLS)


def finish_kernel(in_ref, out_ref):
    def member(m, _):
        block = in_ref[pl.ds(m, COLS, stride=PER_MEM), :].T
        for r in range(ROWS):
            out_ref[pl.ds(m * CELL_ROWS + r, LEVELS, stride=ROWS), :] = block[r * LEVELS : (r + 1) * LEVELS]
        return 0

    lax.fori_loop(0, PER_MEM, member, 0)


SMEM = pl.BlockSpec(memory_space=pltpu.SMEM)
VMEM = pl.BlockSpec(memory_space=pltpu.VMEM)


def shards(prior, north, east, mix, obs_cell, obs_value, obs_var, tile_list, tile_count):
    dom, mem = lax.axis_index("dom"), lax.axis_index("mem")
    where = jnp.stack([dom, mem]).astype(jnp.int32)
    own = tile_list.reshape(SLOT_ROWS, COLS)
    lists = own
    for bit in range(4):
        other = lax.ppermute(lists, "mem", [(i, i ^ (1 << bit)) for i in range(PER_MEM)])
        lists = jnp.concatenate([lists, other], axis=0)

    meta = jnp.concatenate([obs_cell.astype(F32), obs_value, obs_var]).reshape(META, COLS)
    packed = jnp.concatenate(
        [prior.reshape(PER_MEM, CELL_ROWS, COLS), jnp.broadcast_to(meta[None], (PER_MEM, META, COLS))], axis=1
    )
    whole = lax.all_to_all(packed, "dom", split_axis=0, concat_axis=0, tiled=True)
    field, near = pl.pallas_call(
        forecast_kernel,
        name="forecast",
        out_shape=(
            jax.ShapeDtypeStruct((STRIPS * PACK, COLS), F32),
            jax.ShapeDtypeStruct((META * 8, COLS), F32),
        ),
        in_specs=[SMEM, SMEM, SMEM, SMEM, VMEM],
        out_specs=(VMEM, VMEM),
        scratch_shapes=[
            pltpu.VMEM((HEIGHT * LEVELS, COLS), F32),
            pltpu.VMEM((HEIGHT * LEVELS, COLS), F32),
            pltpu.VMEM((HEIGHT * LEVELS, COLS), F32),
            pltpu.VMEM((STRIPS * OBS_CHUNKS, COLS), F32),
        ],
    )(where, north, east, mix, whole.reshape(STRIPS * PACK, COLS))
    strip = lax.all_to_all(
        field.reshape(STRIPS, PACK, COLS), "dom", split_axis=0, concat_axis=0, tiled=True
    )
    sent = pl.pallas_call(
        select_kernel,
        name="select",
        out_shape=jax.ShapeDtypeStruct((PER_MEM * SEND * PER_MEM, COLS), F32),
        in_specs=[SMEM, VMEM, VMEM],
        out_specs=VMEM,
        scratch_shapes=[pltpu.VMEM((META * PER_MEM, COLS), F32)],
    )(where, lists, strip.reshape(PER_MEM * PACK, COLS))
    tiles = lax.all_to_all(
        sent.reshape(PER_MEM, SEND * PER_MEM, COLS), "mem", split_axis=0, concat_axis=0, tiled=True
    )
    updated = pl.pallas_call(
        update_kernel,
        name="update",
        out_shape=jax.ShapeDtypeStruct((PER_MEM, COLS_HERE, PER_MEM, COLS), F32),
        in_specs=[SMEM, SMEM, VMEM, VMEM, VMEM],
        out_specs=VMEM,
        scratch_shapes=[pltpu.VMEM((2, 256, 256), F32), pltpu.VMEM((2, 256, 256), F32)],
    )(where, tile_count, own, near, tiles.reshape(PER_MEM, SEND, PER_MEM, COLS))
    back = lax.all_to_all(
        updated.reshape(PER_MEM, COLS_HERE * PER_MEM, COLS), "mem", split_axis=0, concat_axis=0, tiled=True
    )
    result = pl.pallas_call(
        finish_kernel,
        name="finish",
        out_shape=jax.ShapeDtypeStruct((PER_MEM * CELL_ROWS, COLS), F32),
        in_specs=[VMEM],
        out_specs=VMEM,
    )(back.reshape(PER_MEM * COLS_HERE * PER_MEM, COLS))
    return result.reshape(PER_MEM, LEVELS, ROWS, COLS)


def solution(mesh):
    placed = (
        P("mem", None, "dom", None),
        P(),
        P(),
        P(),
        P("dom"),
        P("dom"),
        P("dom"),
        P("dom", "mem", None),
        P("dom", "mem"),
    )
    return jax.shard_map(
        shards, mesh=mesh, in_specs=placed, out_specs=P("mem", None, "dom", None), check_vma=False
    )
```

```python
import jax
import jax.numpy as jnp
from jax import lax
from jax.experimental import pallas as pl
from jax.experimental.pallas import tpu as pltpu
from jax.sharding import PartitionSpec as P

LOC = 8
STEPS = 3
NS_ITERS = 5
INFLATION = 1.1

F32 = jnp.float32
BF16 = jnp.bfloat16
LEVELS = 32
ROWS = 4
COLS = 128
CELL_ROWS = LEVELS * ROWS
OBS_CHUNKS = 8
META = 3 * OBS_CHUNKS
PACK = CELL_ROWS + META
SLOT_ROWS = 4
COLS_HERE = 8
SEND = COLS_HERE + SLOT_ROWS
PER_MEM = 16
STRIPS = 16
HEIGHT = STRIPS * ROWS


def lane_gather(values, lanes):
    return jnp.take_along_axis(values, lanes, axis=1, mode="promise_in_bounds")


def forecast_kernel(where_ref, north_ref, east_ref, mix_ref, in_ref, list_ref, out_ref, meta_ref, q_ref, t1_ref, t2_ref, hx_ref):
    def load(s, _):
        for r in range(ROWS):
            q_ref[pl.ds(s * CELL_ROWS + r * LEVELS, LEVELS), :] = in_ref[
                pl.ds(s * PACK + r, LEVELS, stride=ROWS), :
            ]
        return 0

    lax.fori_loop(0, STRIPS, load, 0)

    def level_group(g, _):
        sub = lax.broadcasted_iota(jnp.int32, (8, COLS), 0)

        def spread(ref):
            value = jnp.full((8, COLS), ref[g * 8], F32)
            for i in range(1, 8):
                value = jnp.where(sub == i, ref[g * 8 + i], value)
            return value

        north, east, mix = spread(north_ref), spread(east_ref), spread(mix_ref)
        up, down = mix - 0.5 * north, mix + 0.5 * north
        right, left = mix - 0.5 * east, mix + 0.5 * east
        mid = -4.0 * mix

        def stage(src, dst, scale):
            a, b, c, d, e = up * scale, down * scale, right * scale, left * scale, mid * scale

            def at(ref, x):
                return ref.at[pl.ds(pl.multiple_of(x * LEVELS + g * 8, 8), 8), :]

            prev, cur = at(src, HEIGHT - 1)[...], at(src, 0)[...]
            first = cur
            for x in range(HEIGHT):
                nxt = first if x == HEIGHT - 1 else at(src, x + 1)[...]
                base = cur if src is q_ref else at(q_ref, x)[...]
                at(dst, x)[...] = (
                    base
                    + (a * nxt + b * prev)
                    + (c * pltpu.roll(cur, COLS - 1, 1) + d * pltpu.roll(cur, 1, 1))
                    + e * cur
                )
                prev, cur = cur, nxt

        def step(_, c):
            stage(q_ref, t1_ref, 1.0 / 3.0)
            stage(t1_ref, t2_ref, 0.5)
            stage(t2_ref, q_ref, 1.0)
            return c

        lax.fori_loop(0, STEPS, step, 0)
        return 0

    lax.fori_loop(0, LEVELS // 8, level_group, 0)

    for g in range(2):
        lanes, rows = [], []
        for j in range(OBS_CHUNKS):
            cell = in_ref[pl.ds(g * 8 * PACK + CELL_ROWS + j, 8, stride=PACK), :].astype(jnp.int32)
            lanes.append(cell & (COLS - 1))
            line = cell >> 7
            rows.append((line & (ROWS - 1)) * LEVELS + (line >> 2))

        def pick(p, acc):
            src = q_ref[pl.ds(p + g * 8 * CELL_ROWS, 8, stride=CELL_ROWS), :]
            return tuple(
                jnp.where(rows[j] == p, lane_gather(src, lanes[j]), acc[j]) for j in range(OBS_CHUNKS)
            )

        acc = lax.fori_loop(
            0, CELL_ROWS, pick, tuple(jnp.zeros((8, COLS), F32) for _ in range(OBS_CHUNKS)), unroll=4
        )
        for j in range(OBS_CHUNKS):
            hx_ref[pl.ds(g * 64 + j, 8, stride=OBS_CHUNKS), :] = acc[j]

    def store(s, _):
        base = pl.multiple_of(s * CELL_ROWS, 8)
        to = pl.multiple_of(s * PACK, 8)
        out_ref[pl.ds(to, CELL_ROWS), :] = q_ref[pl.ds(base, CELL_ROWS), :].T
        for t in range(3):
            strip = lax.rem(s + STRIPS - 1 + t, STRIPS)
            out_ref[pl.ds(to + CELL_ROWS + 8 * t, 8), :] = hx_ref[pl.ds(pl.multiple_of(strip * 8, 8), 8), :]
        return 0

    lax.fori_loop(0, STRIPS, store, 0)

    meta_ref[...] = jnp.zeros_like(meta_ref)
    for t in range(3):
        strip = lax.rem(where_ref[0] + STRIPS - 1 + t, STRIPS)
        for which in range(3):
            meta_ref[pl.ds(t * 64 + which, 8, stride=8), :] = in_ref[
                pl.ds(pl.multiple_of(strip * PACK + CELL_ROWS + which * 8, 8), 8), :
            ]


def select_kernel(where_ref, list_ref, in_ref, out_ref, d_ref):
    for j in range(META):
        d_ref[pl.ds(j * PER_MEM, PER_MEM), :] = in_ref[pl.ds(CELL_ROWS + j, PER_MEM, stride=PACK), :]

    def peer(kb, _):
        to = pl.multiple_of(kb * SEND * PER_MEM, 8)
        for c in range(COLS_HERE):
            out_ref[pl.ds(to + c * PER_MEM, PER_MEM), :] = in_ref[
                pl.ds(kb * COLS_HERE + c, PER_MEM, stride=PACK), :
            ]
        first = lax.bitwise_xor(where_ref[1], kb) * SLOT_ROWS
        for q in range(SLOT_ROWS):
            slot = jnp.broadcast_to(list_ref[pl.ds(first + q, 1), :], (8, COLS))
            lanes = slot & (COLS - 1)
            chunk = slot >> 7
            low = jnp.zeros((8, COLS), F32)
            high = jnp.zeros((8, COLS), F32)
            for j in range(META):
                here = chunk == j
                low = jnp.where(here, lane_gather(d_ref[pl.ds(j * PER_MEM, 8), :], lanes), low)
                high = jnp.where(here, lane_gather(d_ref[pl.ds(j * PER_MEM + 8, 8), :], lanes), high)
            at = to + (COLS_HERE + q) * PER_MEM
            out_ref[pl.ds(at, 8), :] = low
            out_ref[pl.ds(at + 8, 8), :] = high
        return 0

    lax.fori_loop(0, PER_MEM, peer, 0)


def parts(x):
    high = x.astype(BF16)
    return high, (x - high.astype(F32)).astype(BF16)


def product(a, b, dims=(((1,), (0,)), ((), ()))):
    def dot(x, y):
        return lax.dot_general(x, y, dims, preferred_element_type=F32)

    return dot(a[0], b[0]) + (dot(a[0], b[1]) + dot(a[1], b[0]))


def update_kernel(where_ref, count_ref, list_ref, meta_ref, in_ref, out_ref, it_ref, root_ref):
    members = 256
    row_id = lax.broadcasted_iota(jnp.int32, (members, members), 0)
    col_id = lax.broadcasted_iota(jnp.int32, (members, members), 1)
    diagonal = row_id == col_id
    slot_id = lax.broadcasted_iota(jnp.int32, (1, COLS), 1)

    def plus_identity(x, scale):
        return jnp.where(diagonal, x + scale, x)

    norms, drives = [], []
    for t in range(2):
        values, rhos, anomalies = [], [], []
        for h in range(2):
            slot = list_ref[pl.ds(2 * t + h, 1), :]
            wide = jnp.broadcast_to(slot, (8, COLS))
            lanes = wide & (COLS - 1)
            chunk = wide >> 7
            found = jnp.zeros((8, COLS), F32)
            for j in range(META):
                found = jnp.where(chunk == j, lane_gather(meta_ref[pl.ds(j * 8, 8), :], lanes), found)
            line = found[0:1].astype(jnp.int32)
            strip = where_ref[0] + STRIPS - 1 + (slot >> 10)
            strip = strip & (STRIPS - 1)
            place_x = (strip * ROWS + ((line >> 7) & (ROWS - 1))).astype(F32)
            place_y = (line & (COLS - 1)).astype(F32)
            centre_x = (where_ref[0] * 4).astype(F32) + 1.5
            centre_y = ((where_ref[1] * 2 + t) * 4).astype(F32) + 1.5
            dx = place_x - centre_x + 0.5 * HEIGHT
            dx = jnp.where(dx >= HEIGHT, dx - HEIGHT, dx)
            dx = jnp.where(dx < 0, dx + HEIGHT, dx) - 0.5 * HEIGHT
            dy = place_y - centre_y + 0.5 * COLS
            dy = jnp.where(dy >= COLS, dy - COLS, dy)
            dy = jnp.where(dy < 0, dy + COLS, dy) - 0.5 * COLS
            live = slot_id + h * COLS < count_ref[0, t]
            spread = found[2:3] * (1.0 + (dx * dx + dy * dy) / float(LOC * LOC))
            rho = jnp.where(live, 1.0 / spread, 0.0)
            obs = in_ref[:, COLS_HERE + 2 * t + h].reshape(members, COLS)
            mean = jnp.sum(obs, axis=0, keepdims=True) * (1.0 / members)
            values.append(found[1:2] - mean)
            rhos.append(rho)
            anomalies.append(obs - mean)
        anomaly = jnp.concatenate(anomalies, axis=1)
        rho = jnp.concatenate(rhos, axis=1)
        innovation = jnp.concatenate(values, axis=1)
        drives.append(jnp.sum(anomaly * (rho * innovation), axis=1, keepdims=True))
        scaled = parts(anomaly * jnp.sqrt(rho))
        gram = product(scaled, scaled, (((1,), (1,)), ((), ())))
        gram = plus_identity(gram, (members - 1) / INFLATION)
        norm = jnp.sqrt(jnp.sum(jnp.sum(gram * gram, axis=1, keepdims=True), axis=0, keepdims=True))
        norms.append(norm)
        it = gram / norm
        factor = plus_identity(-0.5 * it, 1.5)
        root_ref[t] = factor
        it_ref[t] = product(parts(it), parts(factor))

    def iteration(_, c):
        for t in range(2):
            root, it = parts(root_ref[t]), parts(it_ref[t])
            factor = parts(plus_identity(-0.5 * product(root, it), 1.5))
            it_ref[t] = product(it, factor)
            root_ref[t] = product(factor, root)
        return c

    lax.fori_loop(0, NS_ITERS - 2, iteration, 0)

    for t in range(2):
        root, it = parts(root_ref[t]), parts(it_ref[t])
        factor = parts(plus_identity(-0.5 * product(root, it), 1.5))
        full = product(factor, root)
        inner = jnp.sum(full * drives[t], axis=0, keepdims=True)
        shift = jnp.sum(full * inner, axis=1, keepdims=True) / norms[t]
        scale = jnp.sqrt((members - 1) / norms[t])
        root = parts(full * scale)
        for c in range(4 * t, 4 * t + 4):
            x = in_ref[:, c].reshape(members, COLS)
            mean = jnp.sum(x, axis=0, keepdims=True) * (1.0 / members)
            x = x - mean
            moved = mean + jnp.sum(x * shift, axis=0, keepdims=True)
            out = product(root, parts(x)) + moved
            out_ref[:, c] = out.reshape(PER_MEM, PER_MEM, COLS)


def finish_kernel(in_ref, out_ref):
    def member(m, _):
        block = in_ref[pl.ds(m, COLS, stride=PER_MEM), :].T
        for r in range(ROWS):
            out_ref[pl.ds(m * CELL_ROWS + r, LEVELS, stride=ROWS), :] = block[r * LEVELS : (r + 1) * LEVELS]
        return 0

    lax.fori_loop(0, PER_MEM, member, 0)


PARAMS = pltpu.CompilerParams(vmem_limit_bytes=20 * 1024 * 1024)
SMEM = pl.BlockSpec(memory_space=pltpu.SMEM)
VMEM = pl.BlockSpec(memory_space=pltpu.VMEM)


def shards(prior, north, east, mix, obs_cell, obs_value, obs_var, tile_list, tile_count):
    dom, mem = lax.axis_index("dom"), lax.axis_index("mem")
    where = jnp.stack([dom, mem]).astype(jnp.int32)
    own = tile_list.reshape(SLOT_ROWS, COLS)
    lists = own
    for bit in range(4):
        other = lax.ppermute(lists, "mem", [(i, i ^ (1 << bit)) for i in range(PER_MEM)])
        lists = jnp.concatenate([lists, other], axis=0)

    meta = jnp.concatenate([obs_cell.astype(F32), obs_value, obs_var]).reshape(META, COLS)
    packed = jnp.concatenate(
        [prior.reshape(PER_MEM, CELL_ROWS, COLS), jnp.broadcast_to(meta[None], (PER_MEM, META, COLS))], axis=1
    )
    whole = lax.all_to_all(packed, "dom", split_axis=0, concat_axis=0, tiled=True)
    field, near = pl.pallas_call(
        forecast_kernel,
        compiler_params=PARAMS,
        name="forecast",
        out_shape=(
            jax.ShapeDtypeStruct((STRIPS * PACK, COLS), F32),
            jax.ShapeDtypeStruct((META * 8, COLS), F32),
        ),
        in_specs=[SMEM, SMEM, SMEM, SMEM, VMEM, pl.BlockSpec(memory_space=pl.ANY)],
        out_specs=(VMEM, VMEM),
        scratch_shapes=[
            pltpu.VMEM((HEIGHT * LEVELS, COLS), F32),
            pltpu.VMEM((HEIGHT * LEVELS, COLS), F32),
            pltpu.VMEM((HEIGHT * LEVELS, COLS), F32),
            pltpu.VMEM((STRIPS * OBS_CHUNKS, COLS), F32),
        ],
    )(where, north, east, mix, whole.reshape(STRIPS * PACK, COLS), lists)
    strip = lax.all_to_all(
        field.reshape(STRIPS, PACK, COLS), "dom", split_axis=0, concat_axis=0, tiled=True
    )
    sent = pl.pallas_call(
        select_kernel,
        compiler_params=PARAMS,
        name="select",
        out_shape=jax.ShapeDtypeStruct((PER_MEM * SEND * PER_MEM, COLS), F32),
        in_specs=[SMEM, VMEM, VMEM],
        out_specs=VMEM,
        scratch_shapes=[pltpu.VMEM((META * PER_MEM, COLS), F32)],
    )(where, lists, strip.reshape(PER_MEM * PACK, COLS))
    tiles = lax.all_to_all(
        sent.reshape(PER_MEM, SEND * PER_MEM, COLS), "mem", split_axis=0, concat_axis=0, tiled=True
    )
    updated = pl.pallas_call(
        update_kernel,
        compiler_params=PARAMS,
        name="update",
        out_shape=jax.ShapeDtypeStruct((PER_MEM, COLS_HERE, PER_MEM, COLS), F32),
        in_specs=[SMEM, SMEM, VMEM, VMEM, VMEM],
        out_specs=VMEM,
        scratch_shapes=[pltpu.VMEM((2, 256, 256), F32), pltpu.VMEM((2, 256, 256), F32)],
    )(where, tile_count, own, near, tiles.reshape(PER_MEM, SEND, PER_MEM, COLS))
    back = lax.all_to_all(
        updated.reshape(PER_MEM, COLS_HERE * PER_MEM, COLS), "mem", split_axis=0, concat_axis=0, tiled=True
    )
    result = pl.pallas_call(
        finish_kernel,
        compiler_params=PARAMS,
        name="finish",
        out_shape=jax.ShapeDtypeStruct((PER_MEM * CELL_ROWS, COLS), F32),
        in_specs=[VMEM],
        out_specs=VMEM,
    )(back.reshape(PER_MEM * COLS_HERE * PER_MEM, COLS))
    return result.reshape(PER_MEM, LEVELS, ROWS, COLS)


def solution(mesh):
    placed = (
        P("mem", None, "dom", None),
        P(),
        P(),
        P(),
        P("dom"),
        P("dom"),
        P("dom"),
        P("dom", "mem", None),
        P("dom", "mem"),
    )
    return jax.shard_map(
        shards, mesh=mesh, in_specs=placed, out_specs=P("mem", None, "dom", None), check_vma=False
    )
```

```python
import jax
import jax.numpy as jnp
from jax import lax
from jax.experimental import pallas as pl
from jax.experimental.pallas import tpu as pltpu
from jax.sharding import PartitionSpec as P

LOC = 8
STEPS = 3
NS_ITERS = 5
INFLATION = 1.1

F32 = jnp.float32
BF16 = jnp.bfloat16
LEVELS = 32
ROWS = 4
COLS = 128
CELL_ROWS = LEVELS * ROWS
OBS_CHUNKS = 8
META = 3 * OBS_CHUNKS
PACK = CELL_ROWS + META
SLOT_ROWS = 4
COLS_HERE = 8
SEND = COLS_HERE + SLOT_ROWS
PER_MEM = 16
STRIPS = 16
HEIGHT = STRIPS * ROWS
PITCH = CELL_ROWS + 8


LANES = lax.GatherDimensionNumbers(
    offset_dims=(),
    collapsed_slice_dims=(1,),
    start_index_map=(1,),
    operand_batching_dims=(0,),
    start_indices_batching_dims=(0,),
)


def lane_gather(values, lanes):
    return lax.gather(
        values, lanes[..., None], LANES, (1, 1), mode=lax.GatherScatterMode.PROMISE_IN_BOUNDS
    )


def pack_kernel(prior_ref, cell_ref, value_ref, var_ref, out_ref, sems):
    def copy(m):
        return pltpu.make_async_copy(
            prior_ref.at[pl.ds(m * CELL_ROWS, CELL_ROWS), :],
            out_ref.at[pl.ds(m * PACK, CELL_ROWS), :],
            sems.at[m],
        )

    for m in range(PER_MEM):
        copy(m).start()
    cell, value, var = cell_ref[...].astype(F32), value_ref[...], var_ref[...]
    for m in range(PER_MEM):
        at = m * PACK + CELL_ROWS
        out_ref[at : at + 8, :] = cell
        out_ref[at + 8 : at + 16, :] = value
        out_ref[at + 16 : at + 24, :] = var
    for m in range(PER_MEM):
        copy(m).wait()


def forecast_kernel(where_ref, north_ref, east_ref, mix_ref, in_ref, out_ref, hx_ref, meta_ref, q_ref, t1_ref, t2_ref):
    def load(s, _):
        for r in range(ROWS):
            q_ref[pl.ds(pl.multiple_of(s * PITCH + r * LEVELS, 8), LEVELS), :] = in_ref[
                pl.ds(s * PACK + r, LEVELS, stride=ROWS), :
            ]
        return 0

    lax.fori_loop(0, STRIPS, load, 0)

    def level_group(g, _):
        sub = lax.broadcasted_iota(jnp.int32, (8, COLS), 0)

        def spread(ref):
            value = jnp.full((8, COLS), ref[g * 8], F32)
            for i in range(1, 8):
                value = jnp.where(sub == i, ref[g * 8 + i], value)
            return value

        north, east, mix = spread(north_ref), spread(east_ref), spread(mix_ref)
        up, down = mix - 0.5 * north, mix + 0.5 * north
        right, left = mix - 0.5 * east, mix + 0.5 * east
        mid = -4.0 * mix

        def stage(src, dst, scale):
            a, b, c, d, e = up * scale, down * scale, right * scale, left * scale, mid * scale

            def at(ref, x):
                at_row = x // ROWS * PITCH + x % ROWS * LEVELS
                return ref.at[pl.ds(pl.multiple_of(at_row + g * 8, 8), 8), :]

            prev, cur = at(src, HEIGHT - 1)[...], at(src, 0)[...]
            first = cur
            for x in range(HEIGHT):
                nxt = first if x == HEIGHT - 1 else at(src, x + 1)[...]
                base = cur if src is q_ref else at(q_ref, x)[...]
                at(dst, x)[...] = (
                    base
                    + (a * nxt + b * prev)
                    + (c * pltpu.roll(cur, COLS - 1, 1) + d * pltpu.roll(cur, 1, 1))
                    + e * cur
                )
                prev, cur = cur, nxt

        def step(_, c):
            stage(q_ref, t1_ref, 1.0 / 3.0)
            stage(t1_ref, t2_ref, 0.5)
            stage(t2_ref, q_ref, 1.0)
            return c

        lax.fori_loop(0, STEPS, step, 0)
        return 0

    lax.fori_loop(0, LEVELS // 8, level_group, 0)

    for g in range(2):
        lanes, rows = [], []
        for j in range(OBS_CHUNKS):
            cell = in_ref[pl.ds(g * 8 * PACK + CELL_ROWS + j, 8, stride=PACK), :].astype(jnp.int32)
            lanes.append(cell & (COLS - 1))
            line = cell >> 7
            rows.append((line & (ROWS - 1)) * LEVELS + (line >> 2))

        def pick(p, acc):
            src = q_ref[pl.ds(p + g * 8 * PITCH, 8, stride=PITCH), :]
            return tuple(
                jnp.where(rows[j] == p, lane_gather(src, lanes[j]), acc[j]) for j in range(OBS_CHUNKS)
            )

        acc = lax.fori_loop(
            0, CELL_ROWS, pick, tuple(jnp.zeros((8, COLS), F32) for _ in range(OBS_CHUNKS)), unroll=16
        )
        for j in range(OBS_CHUNKS):
            hx_ref[pl.ds(g * 64 + j, 8, stride=OBS_CHUNKS), :] = acc[j]

    def store(s, _):
        base = pl.multiple_of(s * PITCH, 8)
        to = pl.multiple_of(s * CELL_ROWS, 8)
        out_ref[pl.ds(to, CELL_ROWS), :] = q_ref[pl.ds(base, CELL_ROWS), :].T
        return 0

    lax.fori_loop(0, STRIPS, store, 0)

    meta_ref[...] = jnp.zeros_like(meta_ref)
    for t in range(3):
        strip = lax.rem(where_ref[0] + STRIPS - 1 + t, STRIPS)
        for which in range(3):
            meta_ref[pl.ds(t * 64 + which, 8, stride=8), :] = in_ref[
                pl.ds(pl.multiple_of(strip * PACK + CELL_ROWS + which * 8, 8), 8), :
            ]


def select_kernel(where_ref, list_ref, hx_ref, in_ref, out_ref):
    def strip(a, _):
        for kb in range(PER_MEM):
            out_ref[pl.ds((kb * STRIPS + a) * SEND, COLS_HERE), :] = in_ref[
                pl.ds(pl.multiple_of(a * CELL_ROWS + kb * COLS_HERE, 8), COLS_HERE), :
            ]
        sources = []
        for t in range(3):
            near = lax.rem(a + STRIPS - 1 + t, STRIPS) * OBS_CHUNKS
            for j in range(OBS_CHUNKS):
                sources.append(jnp.broadcast_to(hx_ref[pl.ds(near + j, 1), :], (8, COLS)))
        for g in range(PER_MEM // 2):
            slot = list_ref[pl.ds(pl.multiple_of(a * PER_MEM * SLOT_ROWS + g * 8, 8), 8), :]
            lanes = slot & (COLS - 1)
            chunk = slot >> 7
            found = lane_gather(sources[0], lanes)
            for j in range(1, META):
                found = jnp.where(chunk == j, lane_gather(sources[j], lanes), found)
            for i in range(2):
                kb = lax.bitwise_xor(where_ref[1], 2 * g + i)
                out_ref[pl.ds((kb * STRIPS + a) * SEND + COLS_HERE, SLOT_ROWS), :] = found[
                    i * SLOT_ROWS : (i + 1) * SLOT_ROWS
                ]
        return 0

    lax.fori_loop(0, STRIPS, strip, 0)


def parts(x):
    high = x.astype(BF16)
    return high, (x - high.astype(F32)).astype(BF16)


def product(a, b, dims=(((1,), (0,)), ((), ()))):
    def dot(x, y):
        return lax.dot_general(x, y, dims, preferred_element_type=F32)

    return dot(a[0], b[0]) + (dot(a[0], b[1]) + dot(a[1], b[0]))


def update_kernel(where_ref, count_ref, list_ref, meta_ref, in_ref, out_ref, it_ref, root_ref):
    members = 256
    row_id = lax.broadcasted_iota(jnp.int32, (members, members), 0)
    col_id = lax.broadcasted_iota(jnp.int32, (members, members), 1)
    diagonal = row_id == col_id
    slot_id = lax.broadcasted_iota(jnp.int32, (1, COLS), 1)

    def plus_identity(x, scale):
        return jnp.where(diagonal, x + scale, x)

    norms, drives = [], []
    for t in range(2):
        values, rhos, anomalies = [], [], []
        for h in range(2):
            slot = list_ref[pl.ds(2 * t + h, 1), :]
            wide = jnp.broadcast_to(slot, (8, COLS))
            lanes = wide & (COLS - 1)
            chunk = wide >> 7
            found = jnp.zeros((8, COLS), F32)
            for j in range(META):
                found = jnp.where(chunk == j, lane_gather(meta_ref[pl.ds(j * 8, 8), :], lanes), found)
            line = found[0:1].astype(jnp.int32)
            strip = where_ref[0] + STRIPS - 1 + (slot >> 10)
            strip = strip & (STRIPS - 1)
            place_x = (strip * ROWS + ((line >> 7) & (ROWS - 1))).astype(F32)
            place_y = (line & (COLS - 1)).astype(F32)
            centre_x = (where_ref[0] * 4).astype(F32) + 1.5
            centre_y = ((where_ref[1] * 2 + t) * 4).astype(F32) + 1.5
            dx = place_x - centre_x + 0.5 * HEIGHT
            dx = jnp.where(dx >= HEIGHT, dx - HEIGHT, dx)
            dx = jnp.where(dx < 0, dx + HEIGHT, dx) - 0.5 * HEIGHT
            dy = place_y - centre_y + 0.5 * COLS
            dy = jnp.where(dy >= COLS, dy - COLS, dy)
            dy = jnp.where(dy < 0, dy + COLS, dy) - 0.5 * COLS
            live = slot_id + h * COLS < count_ref[0, t]
            spread = found[2:3] * (1.0 + (dx * dx + dy * dy) / float(LOC * LOC))
            rho = jnp.where(live, 1.0 / spread, 0.0)
            obs = in_ref[pl.ds(COLS_HERE + 2 * t + h, members, stride=SEND), :]
            mean = jnp.sum(obs, axis=0, keepdims=True) * (1.0 / members)
            values.append(found[1:2] - mean)
            rhos.append(rho)
            anomalies.append(obs - mean)
        anomaly = jnp.concatenate(anomalies, axis=1)
        rho = jnp.concatenate(rhos, axis=1)
        innovation = jnp.concatenate(values, axis=1)
        drives.append(jnp.sum(anomaly * (rho * innovation), axis=1, keepdims=True))
        scaled = parts(anomaly * jnp.sqrt(rho))
        gram = product(scaled, scaled, (((1,), (1,)), ((), ())))
        gram = plus_identity(gram, (members - 1) / INFLATION)
        norm = jnp.sqrt(jnp.sum(jnp.sum(gram * gram, axis=1, keepdims=True), axis=0, keepdims=True))
        norms.append(norm)
        it = gram / norm
        factor = plus_identity(-0.5 * it, 1.5)
        root_ref[t] = factor
        it_ref[t] = product(parts(it), parts(factor))

    def iteration(_, c):
        for t in range(2):
            root, it = parts(root_ref[t]), parts(it_ref[t])
            factor = parts(plus_identity(-0.5 * product(root, it), 1.5))
            it_ref[t] = product(it, factor)
            root_ref[t] = product(factor, root)
        return c

    lax.fori_loop(0, NS_ITERS - 2, iteration, 0)

    for t in range(2):
        root, it = parts(root_ref[t]), parts(it_ref[t])
        factor = parts(plus_identity(-0.5 * product(root, it), 1.5))
        full = product(factor, root)
        inner = jnp.sum(full * drives[t], axis=0, keepdims=True)
        shift = jnp.sum(full * inner, axis=1, keepdims=True) / norms[t]
        scale = jnp.sqrt((members - 1) / norms[t])
        root = parts(full * scale)
        for c in range(4 * t, 4 * t + 4):
            x = in_ref[pl.ds(c, members, stride=SEND), :]
            mean = jnp.sum(x, axis=0, keepdims=True) * (1.0 / members)
            x = x - mean
            moved = mean + jnp.sum(x * shift, axis=0, keepdims=True)
            out = product(root, parts(x)) + moved
            out_ref[:, c] = out.reshape(PER_MEM, PER_MEM, COLS)


def finish_kernel(in_ref, out_ref):
    def member(m, _):
        block = in_ref[pl.ds(m, COLS, stride=PER_MEM), :].T
        for r in range(ROWS):
            out_ref[pl.ds(m * CELL_ROWS + r, LEVELS, stride=ROWS), :] = block[r * LEVELS : (r + 1) * LEVELS]
        return 0

    lax.fori_loop(0, PER_MEM, member, 0)


PARAMS = pltpu.CompilerParams(vmem_limit_bytes=20 * 1024 * 1024)
SMEM = pl.BlockSpec(memory_space=pltpu.SMEM)
VMEM = pl.BlockSpec(memory_space=pltpu.VMEM)


def shards(prior, north, east, mix, obs_cell, obs_value, obs_var, tile_list, tile_count):
    dom, mem = lax.axis_index("dom"), lax.axis_index("mem")
    where = jnp.stack([dom, mem]).astype(jnp.int32)
    own = tile_list.reshape(SLOT_ROWS, COLS)
    lists = own
    for bit in range(4):
        other = lax.ppermute(lists, "mem", [(i, i ^ (1 << bit)) for i in range(PER_MEM)])
        lists = jnp.concatenate([lists, other], axis=0)

    packed = pl.pallas_call(
        pack_kernel,
        compiler_params=PARAMS,
        name="pack",
        out_shape=jax.ShapeDtypeStruct((PER_MEM * PACK, COLS), F32),
        in_specs=[pl.BlockSpec(memory_space=pl.ANY), VMEM, VMEM, VMEM],
        out_specs=VMEM,
        scratch_shapes=[pltpu.SemaphoreType.DMA((PER_MEM,))],
    )(
        prior.reshape(PER_MEM * CELL_ROWS, COLS),
        obs_cell.reshape(OBS_CHUNKS, COLS),
        obs_value.reshape(OBS_CHUNKS, COLS),
        obs_var.reshape(OBS_CHUNKS, COLS),
    )
    whole = lax.all_to_all(
        packed.reshape(PER_MEM, PACK, COLS), "dom", split_axis=0, concat_axis=0, tiled=True
    )
    every = lax.all_to_all(
        jnp.broadcast_to(lists[None], (STRIPS, PER_MEM * SLOT_ROWS, COLS)),
        "dom", split_axis=0, concat_axis=0, tiled=True,
    )
    field, hx, near = pl.pallas_call(
        forecast_kernel,
        compiler_params=PARAMS,
        cost_estimate=pl.CostEstimate(flops=30_000_000, bytes_accessed=60_000_000, transcendentals=0),
        name="forecast",
        out_shape=(
            jax.ShapeDtypeStruct((STRIPS * CELL_ROWS, COLS), F32),
            jax.ShapeDtypeStruct((STRIPS * OBS_CHUNKS, COLS), F32),
            jax.ShapeDtypeStruct((META * 8, COLS), F32),
        ),
        in_specs=[SMEM, SMEM, SMEM, SMEM, VMEM],
        out_specs=(VMEM, VMEM, VMEM),
        scratch_shapes=[pltpu.VMEM((STRIPS * PITCH, COLS), F32)] * 3,
    )(where, north, east, mix, whole.reshape(STRIPS * PACK, COLS))
    sent = pl.pallas_call(
        select_kernel,
        compiler_params=PARAMS,
        name="select",
        out_shape=jax.ShapeDtypeStruct((PER_MEM * STRIPS * SEND, COLS), F32),
        in_specs=[SMEM, VMEM, VMEM, VMEM],
        out_specs=VMEM,
    )(where, every.reshape(STRIPS * PER_MEM * SLOT_ROWS, COLS), hx, field)
    tiles = lax.all_to_all(
        sent.reshape(PER_MEM * STRIPS, SEND // 4, 4, COLS),
        ("mem", "dom"), split_axis=0, concat_axis=0, tiled=True,
    )
    updated = pl.pallas_call(
        update_kernel,
        compiler_params=PARAMS,
        name="update",
        out_shape=jax.ShapeDtypeStruct((PER_MEM, COLS_HERE, PER_MEM, COLS), F32),
        in_specs=[SMEM, SMEM, VMEM, VMEM, VMEM],
        out_specs=VMEM,
        scratch_shapes=[pltpu.VMEM((2, 256, 256), F32), pltpu.VMEM((2, 256, 256), F32)],
    )(where, tile_count, own, near, tiles.reshape(PER_MEM * STRIPS * SEND, COLS))
    back = lax.all_to_all(
        updated.reshape(PER_MEM, COLS_HERE * PER_MEM, COLS), "mem", split_axis=0, concat_axis=0, tiled=True
    )
    result = pl.pallas_call(
        finish_kernel,
        compiler_params=PARAMS,
        name="finish",
        out_shape=jax.ShapeDtypeStruct((PER_MEM * CELL_ROWS, COLS), F32),
        in_specs=[VMEM],
        out_specs=VMEM,
    )(back.reshape(PER_MEM * COLS_HERE * PER_MEM, COLS))
    return result.reshape(PER_MEM, LEVELS, ROWS, COLS)


def solution(mesh):
    placed = (
        P("mem", None, "dom", None),
        P(),
        P(),
        P(),
        P("dom"),
        P("dom"),
        P("dom"),
        P("dom", "mem", None),
        P("dom", "mem"),
    )
    return jax.shard_map(
        shards, mesh=mesh, in_specs=placed, out_specs=P("mem", None, "dom", None), check_vma=False
    )
```

```python
import jax
import jax.numpy as jnp
from jax import lax
from jax.experimental import pallas as pl
from jax.experimental.pallas import tpu as pltpu
from jax.sharding import PartitionSpec as P

LOC = 8
STEPS = 3
NS_ITERS = 5
INFLATION = 1.1

F32 = jnp.float32
BF16 = jnp.bfloat16
LEVELS = 32
ROWS = 4
COLS = 128
CELL_ROWS = LEVELS * ROWS
OBS_CHUNKS = 8
META = 3 * OBS_CHUNKS
SLOT_ROWS = 4
COLS_HERE = 8
SEND = COLS_HERE + SLOT_ROWS
PER_MEM = 16
STRIPS = 16
HEIGHT = STRIPS * ROWS
PITCH = CELL_ROWS + 8
LISTS = PER_MEM * SLOT_ROWS
AUX = LISTS + META


LANES = lax.GatherDimensionNumbers(
    offset_dims=(),
    collapsed_slice_dims=(1,),
    start_index_map=(1,),
    operand_batching_dims=(0,),
    start_indices_batching_dims=(0,),
)


def lane_gather(values, lanes):
    return lax.gather(
        values, lanes[..., None], LANES, (1, 1), mode=lax.GatherScatterMode.PROMISE_IN_BOUNDS
    )


def aux_kernel(own_ref, l1_ref, l2_ref, l3_ref, l4_ref, cell_ref, value_ref, var_ref, out_ref):
    parts_in = [own_ref, l1_ref, l2_ref, l3_ref, l4_ref, cell_ref, value_ref, var_ref]
    for s in range(STRIPS):
        at = s * AUX
        for ref in parts_in:
            rows = ref.shape[0]
            out_ref[at : at + rows, :] = ref[...].astype(F32)
            at += rows


def forecast_kernel(north_ref, east_ref, mix_ref, in_ref, q_ref, t1_ref, t2_ref):
    def load(s, _):
        for r in range(ROWS):
            q_ref[pl.ds(pl.multiple_of(s * PITCH + r * LEVELS, 8), LEVELS), :] = in_ref[
                pl.ds(s * CELL_ROWS + r, LEVELS, stride=ROWS), :
            ]
        return 0

    lax.fori_loop(0, STRIPS, load, 0, unroll=4)

    def level_group(g, _):
        sub = lax.broadcasted_iota(jnp.int32, (8, COLS), 0)

        def spread(ref):
            value = jnp.full((8, COLS), ref[g * 8], F32)
            for i in range(1, 8):
                value = jnp.where(sub == i, ref[g * 8 + i], value)
            return value

        north, east, mix = spread(north_ref), spread(east_ref), spread(mix_ref)
        up, down = mix - 0.5 * north, mix + 0.5 * north
        right, left = mix - 0.5 * east, mix + 0.5 * east
        mid = -4.0 * mix

        def stage(src, dst, scale):
            a, b, c, d, e = up * scale, down * scale, right * scale, left * scale, mid * scale

            def at(ref, x):
                at_row = x // ROWS * PITCH + x % ROWS * LEVELS
                return ref.at[pl.ds(pl.multiple_of(at_row + g * 8, 8), 8), :]

            prev, cur = at(src, HEIGHT - 1)[...], at(src, 0)[...]
            first = cur
            for x in range(HEIGHT):
                nxt = first if x == HEIGHT - 1 else at(src, x + 1)[...]
                base = cur if src is q_ref else at(q_ref, x)[...]
                at(dst, x)[...] = (
                    base
                    + (a * nxt + b * prev)
                    + (c * pltpu.roll(cur, COLS - 1, 1) + d * pltpu.roll(cur, 1, 1))
                    + e * cur
                )
                prev, cur = cur, nxt

        def step(_, c):
            stage(q_ref, t1_ref, 1.0 / 3.0)
            stage(t1_ref, t2_ref, 0.5)
            stage(t2_ref, q_ref, 1.0)
            return c

        lax.fori_loop(0, STEPS, step, 0)
        return 0

    lax.fori_loop(0, LEVELS // 8, level_group, 0)


def select_kernel(where_ref, aux_ref, q_ref, out_ref, meta_ref, hx_ref):
    for g in range(2):
        lanes, rows = [], []
        for j in range(OBS_CHUNKS):
            cell = aux_ref[pl.ds(g * 8 * AUX + LISTS + j, 8, stride=AUX), :].astype(jnp.int32)
            lanes.append(cell & (COLS - 1))
            line = cell >> 7
            rows.append((line & (ROWS - 1)) * LEVELS + (line >> 2))

        def pick(p, acc):
            src = q_ref[pl.ds(p + g * 8 * PITCH, 8, stride=PITCH), :]
            return tuple(
                jnp.where(rows[j] == p, lane_gather(src, lanes[j]), acc[j]) for j in range(OBS_CHUNKS)
            )

        acc = lax.fori_loop(
            0, CELL_ROWS, pick, tuple(jnp.zeros((8, COLS), F32) for _ in range(OBS_CHUNKS)), unroll=16
        )
        for j in range(OBS_CHUNKS):
            hx_ref[pl.ds(g * 64 + j, 8, stride=OBS_CHUNKS), :] = acc[j]

    def strip(a, _):
        columns = q_ref[pl.ds(pl.multiple_of(a * PITCH, 8), CELL_ROWS), :].T
        for kb in range(PER_MEM):
            out_ref[pl.ds((kb * STRIPS + a) * SEND, COLS_HERE), :] = columns[
                kb * COLS_HERE : (kb + 1) * COLS_HERE
            ]
        sources = []
        for t in range(3):
            near = lax.rem(a + STRIPS - 1 + t, STRIPS) * OBS_CHUNKS
            for j in range(OBS_CHUNKS):
                sources.append(jnp.broadcast_to(hx_ref[pl.ds(near + j, 1), :], (8, COLS)))
        for g in range(PER_MEM // 2):
            slot = aux_ref[pl.ds(pl.multiple_of(a * AUX + g * 8, 8), 8), :].astype(jnp.int32)
            lanes = slot & (COLS - 1)
            chunk = slot >> 7
            found = lane_gather(sources[0], lanes)
            for j in range(1, META):
                found = jnp.where(chunk == j, lane_gather(sources[j], lanes), found)
            for i in range(2):
                kb = lax.bitwise_xor(where_ref[1], 2 * g + i)
                out_ref[pl.ds((kb * STRIPS + a) * SEND + COLS_HERE, SLOT_ROWS), :] = found[
                    i * SLOT_ROWS : (i + 1) * SLOT_ROWS
                ]
        return 0

    lax.fori_loop(0, STRIPS, strip, 0)

    meta_ref[...] = jnp.zeros_like(meta_ref)
    for t in range(3):
        strip = lax.rem(where_ref[0] + STRIPS - 1 + t, STRIPS)
        for which in range(3):
            meta_ref[pl.ds(t * 64 + which, 8, stride=8), :] = aux_ref[
                pl.ds(pl.multiple_of(strip * AUX + LISTS + which * 8, 8), 8), :
            ]


def parts(x):
    high = x.astype(BF16)
    return high, (x - high.astype(F32)).astype(BF16)


def product(a, b, dims=(((1,), (0,)), ((), ()))):
    def dot(x, y):
        return lax.dot_general(x, y, dims, preferred_element_type=F32)

    return dot(a[0], b[0]) + (dot(a[0], b[1]) + dot(a[1], b[0]))


def update_kernel(where_ref, count_ref, list_ref, meta_ref, in_ref, out_ref, it_ref, root_ref):
    members = 256
    row_id = lax.broadcasted_iota(jnp.int32, (members, members), 0)
    col_id = lax.broadcasted_iota(jnp.int32, (members, members), 1)
    diagonal = row_id == col_id
    slot_id = lax.broadcasted_iota(jnp.int32, (1, COLS), 1)

    def plus_identity(x, scale):
        return jnp.where(diagonal, x + scale, x)

    norms, drives = [], []
    for t in range(2):
        values, rhos, anomalies = [], [], []
        for h in range(2):
            slot = list_ref[pl.ds(2 * t + h, 1), :]
            wide = jnp.broadcast_to(slot, (8, COLS))
            lanes = wide & (COLS - 1)
            chunk = wide >> 7
            found = jnp.zeros((8, COLS), F32)
            for j in range(META):
                found = jnp.where(chunk == j, lane_gather(meta_ref[pl.ds(j * 8, 8), :], lanes), found)
            line = found[0:1].astype(jnp.int32)
            strip = where_ref[0] + STRIPS - 1 + (slot >> 10)
            strip = strip & (STRIPS - 1)
            place_x = (strip * ROWS + ((line >> 7) & (ROWS - 1))).astype(F32)
            place_y = (line & (COLS - 1)).astype(F32)
            centre_x = (where_ref[0] * 4).astype(F32) + 1.5
            centre_y = ((where_ref[1] * 2 + t) * 4).astype(F32) + 1.5
            dx = place_x - centre_x + 0.5 * HEIGHT
            dx = jnp.where(dx >= HEIGHT, dx - HEIGHT, dx)
            dx = jnp.where(dx < 0, dx + HEIGHT, dx) - 0.5 * HEIGHT
            dy = place_y - centre_y + 0.5 * COLS
            dy = jnp.where(dy >= COLS, dy - COLS, dy)
            dy = jnp.where(dy < 0, dy + COLS, dy) - 0.5 * COLS
            live = slot_id + h * COLS < count_ref[0, t]
            spread = found[2:3] * (1.0 + (dx * dx + dy * dy) / float(LOC * LOC))
            rho = jnp.where(live, 1.0 / spread, 0.0)
            obs = in_ref[pl.ds(COLS_HERE + 2 * t + h, members, stride=SEND), :]
            mean = jnp.sum(obs, axis=0, keepdims=True) * (1.0 / members)
            values.append(found[1:2] - mean)
            rhos.append(rho)
            anomalies.append(obs - mean)
        anomaly = jnp.concatenate(anomalies, axis=1)
        rho = jnp.concatenate(rhos, axis=1)
        innovation = jnp.concatenate(values, axis=1)
        drives.append(jnp.sum(anomaly * (rho * innovation), axis=1, keepdims=True))
        scaled = parts(anomaly * jnp.sqrt(rho))
        gram = product(scaled, scaled, (((1,), (1,)), ((), ())))
        gram = plus_identity(gram, (members - 1) / INFLATION)
        norm = jnp.sqrt(jnp.sum(jnp.sum(gram * gram, axis=1, keepdims=True), axis=0, keepdims=True))
        norms.append(norm)
        it = gram / norm
        factor = plus_identity(-0.5 * it, 1.5)
        root_ref[t] = factor
        it_ref[t] = product(parts(it), parts(factor))

    def iteration(_, c):
        for t in range(2):
            root, it = parts(root_ref[t]), parts(it_ref[t])
            factor = parts(plus_identity(-0.5 * product(root, it), 1.5))
            it_ref[t] = product(it, factor)
            root_ref[t] = product(factor, root)
        return c

    lax.fori_loop(0, NS_ITERS - 2, iteration, 0)

    for t in range(2):
        root, it = parts(root_ref[t]), parts(it_ref[t])
        factor = parts(plus_identity(-0.5 * product(root, it), 1.5))
        full = product(factor, root)
        inner = jnp.sum(full * drives[t], axis=0, keepdims=True)
        shift = jnp.sum(full * inner, axis=1, keepdims=True) / norms[t]
        scale = jnp.sqrt((members - 1) / norms[t])
        root = parts(full * scale)
        for c in range(4 * t, 4 * t + 4):
            x = in_ref[pl.ds(c, members, stride=SEND), :]
            mean = jnp.sum(x, axis=0, keepdims=True) * (1.0 / members)
            x = x - mean
            moved = mean + jnp.sum(x * shift, axis=0, keepdims=True)
            out = product(root, parts(x)) + moved
            out_ref[:, c] = out.reshape(PER_MEM, PER_MEM, COLS)


def finish_kernel(in_ref, out_ref):
    def member(m, _):
        block = in_ref[pl.ds(m, COLS, stride=PER_MEM), :].T
        for r in range(ROWS):
            out_ref[pl.ds(m * CELL_ROWS + r, LEVELS, stride=ROWS), :] = block[r * LEVELS : (r + 1) * LEVELS]
        return 0

    lax.fori_loop(0, PER_MEM, member, 0, unroll=4)


PARAMS = pltpu.CompilerParams(vmem_limit_bytes=20 * 1024 * 1024)
SMEM = pl.BlockSpec(memory_space=pltpu.SMEM)
VMEM = pl.BlockSpec(memory_space=pltpu.VMEM)


def shards(prior, north, east, mix, obs_cell, obs_value, obs_var, tile_list, tile_count):
    dom, mem = lax.axis_index("dom"), lax.axis_index("mem")
    where = jnp.stack([dom, mem]).astype(jnp.int32)
    own = tile_list.reshape(SLOT_ROWS, COLS)
    pieces = [own]
    for bit in range(4):
        pairs = [(i, i ^ (1 << bit)) for i in range(PER_MEM)]
        pieces.append(lax.ppermute(jnp.concatenate(pieces, axis=0), "mem", pairs))
    whole = lax.all_to_all(
        prior.reshape(PER_MEM, CELL_ROWS, COLS), "dom", split_axis=0, concat_axis=0, tiled=True
    )
    aux = pl.pallas_call(
        aux_kernel,
        compiler_params=PARAMS,
        name="aux",
        out_shape=jax.ShapeDtypeStruct((STRIPS * AUX, COLS), F32),
        in_specs=[VMEM] * 8,
        out_specs=VMEM,
    )(
        *pieces,
        obs_cell.reshape(OBS_CHUNKS, COLS),
        obs_value.reshape(OBS_CHUNKS, COLS),
        obs_var.reshape(OBS_CHUNKS, COLS),
    )
    every = lax.all_to_all(
        aux.reshape(STRIPS, AUX, COLS), "dom", split_axis=0, concat_axis=0, tiled=True
    )
    levels = pl.pallas_call(
        forecast_kernel,
        compiler_params=PARAMS,
        cost_estimate=pl.CostEstimate(flops=30_000_000, bytes_accessed=60_000_000, transcendentals=0),
        name="forecast",
        out_shape=jax.ShapeDtypeStruct((STRIPS * PITCH, COLS), F32),
        in_specs=[SMEM, SMEM, SMEM, VMEM],
        out_specs=VMEM,
        scratch_shapes=[pltpu.VMEM((STRIPS * PITCH, COLS), F32)] * 2,
    )(north, east, mix, whole.reshape(STRIPS * CELL_ROWS, COLS))
    sent, near = pl.pallas_call(
        select_kernel,
        compiler_params=PARAMS,
        name="select",
        out_shape=(
            jax.ShapeDtypeStruct((PER_MEM * STRIPS * SEND, COLS), F32),
            jax.ShapeDtypeStruct((META * 8, COLS), F32),
        ),
        in_specs=[SMEM, VMEM, VMEM],
        out_specs=(VMEM, VMEM),
        scratch_shapes=[pltpu.VMEM((STRIPS * OBS_CHUNKS, COLS), F32)],
    )(where, every.reshape(STRIPS * AUX, COLS), levels)
    tiles = lax.all_to_all(
        sent.reshape(PER_MEM * STRIPS, SEND // 4, 4, COLS),
        ("mem", "dom"), split_axis=0, concat_axis=0, tiled=True,
    )
    updated = pl.pallas_call(
        update_kernel,
        compiler_params=PARAMS,
        name="update",
        out_shape=jax.ShapeDtypeStruct((PER_MEM, COLS_HERE, PER_MEM, COLS), F32),
        in_specs=[SMEM, SMEM, VMEM, VMEM, VMEM],
        out_specs=VMEM,
        scratch_shapes=[pltpu.VMEM((2, 256, 256), F32), pltpu.VMEM((2, 256, 256), F32)],
    )(where, tile_count, own, near, tiles.reshape(PER_MEM * STRIPS * SEND, COLS))
    back = lax.all_to_all(
        updated.reshape(PER_MEM, COLS_HERE * PER_MEM, COLS), "mem", split_axis=0, concat_axis=0, tiled=True
    )
    result = pl.pallas_call(
        finish_kernel,
        compiler_params=PARAMS,
        name="finish",
        out_shape=jax.ShapeDtypeStruct((PER_MEM * CELL_ROWS, COLS), F32),
        in_specs=[VMEM],
        out_specs=VMEM,
    )(back.reshape(PER_MEM * COLS_HERE * PER_MEM, COLS))
    return result.reshape(PER_MEM, LEVELS, ROWS, COLS)


def solution(mesh):
    placed = (
        P("mem", None, "dom", None),
        P(),
        P(),
        P(),
        P("dom"),
        P("dom"),
        P("dom"),
        P("dom", "mem", None),
        P("dom", "mem"),
    )
    return jax.shard_map(
        shards, mesh=mesh, in_specs=placed, out_specs=P("mem", None, "dom", None), check_vma=False
    )
```

```python
import jax
import jax.numpy as jnp
from jax import lax
from jax.experimental import pallas as pl
from jax.experimental.pallas import tpu as pltpu
from jax.sharding import PartitionSpec as P

LOC = 8
STEPS = 3
NS_ITERS = 5
INFLATION = 1.1

F32 = jnp.float32
BF16 = jnp.bfloat16
LEVELS = 32
ROWS = 4
COLS = 128
CELL_ROWS = LEVELS * ROWS
OBS_CHUNKS = 8
META = 3 * OBS_CHUNKS
SLOT_ROWS = 4
COLS_HERE = 8
SEND = COLS_HERE + SLOT_ROWS
PER_MEM = 16
STRIPS = 16
HEIGHT = STRIPS * ROWS
PITCH = CELL_ROWS + 8
FIELD = STRIPS * PITCH
LISTS = PER_MEM * SLOT_ROWS
AUX = LISTS + META


LANES = lax.GatherDimensionNumbers(
    offset_dims=(),
    collapsed_slice_dims=(1,),
    start_index_map=(1,),
    operand_batching_dims=(0,),
    start_indices_batching_dims=(0,),
)


def lane_gather(values, lanes):
    return lax.gather(
        values, lanes[..., None], LANES, (1, 1), mode=lax.GatherScatterMode.PROMISE_IN_BOUNDS
    )


ARRIVAL = (0, 1, 7, 3, 4, 2, 5, 6)


def aux_kernel(own_ref, l1_ref, l2_ref, l3_ref, l4_ref, cell_ref, value_ref, var_ref, out_ref):
    parts_in = [own_ref, l1_ref, l2_ref, l3_ref, l4_ref, cell_ref, value_ref, var_ref]
    for s in range(STRIPS):
        at = s * AUX
        for ref in parts_in:
            rows = ref.shape[0]
            out_ref[at : at + rows, :] = ref[...].astype(F32)
            at += rows


def forecast_kernel(north_ref, east_ref, mix_ref, in_ref, q_ref, t1_ref, t2_ref):
    def load(s, _):
        for r in range(ROWS):
            q_ref[pl.ds(pl.multiple_of(s * PITCH + r * LEVELS, 8), LEVELS), :] = in_ref[
                pl.ds(s * CELL_ROWS + r, LEVELS, stride=ROWS), :
            ]
        return 0

    lax.fori_loop(0, STRIPS, load, 0, unroll=4)

    def level_group(g, _):
        sub = lax.broadcasted_iota(jnp.int32, (8, COLS), 0)

        def spread(ref):
            value = jnp.full((8, COLS), ref[g * 8], F32)
            for i in range(1, 8):
                value = jnp.where(sub == i, ref[g * 8 + i], value)
            return value

        north, east, mix = spread(north_ref), spread(east_ref), spread(mix_ref)
        up, down = mix - 0.5 * north, mix + 0.5 * north
        right, left = mix - 0.5 * east, mix + 0.5 * east
        mid = -4.0 * mix

        def stage(src, dst, scale):
            a, b, c, d, e = up * scale, down * scale, right * scale, left * scale, mid * scale

            def at(ref, x):
                at_row = x // ROWS * PITCH + x % ROWS * LEVELS
                return ref.at[pl.ds(pl.multiple_of(at_row + g * 8, 8), 8), :]

            prev, cur = at(src, HEIGHT - 1)[...], at(src, 0)[...]
            first = cur
            for x in range(HEIGHT):
                nxt = first if x == HEIGHT - 1 else at(src, x + 1)[...]
                base = cur if src is q_ref else at(q_ref, x)[...]
                at(dst, x)[...] = (
                    base
                    + (a * nxt + b * prev)
                    + (c * pltpu.roll(cur, COLS - 1, 1) + d * pltpu.roll(cur, 1, 1))
                    + e * cur
                )
                prev, cur = cur, nxt

        def step(_, c):
            stage(q_ref, t1_ref, 1.0 / 3.0)
            stage(t1_ref, t2_ref, 0.5)
            stage(t2_ref, q_ref, 1.0)
            return c

        lax.fori_loop(0, STEPS, step, 0)
        return 0

    lax.fori_loop(0, LEVELS // 8, level_group, 0)

    def turn(s, _):
        q_ref[pl.ds(pl.multiple_of(FIELD + s * CELL_ROWS, 8), CELL_ROWS), :] = q_ref[
            pl.ds(pl.multiple_of(s * PITCH, 8), CELL_ROWS), :
        ].T
        return 0

    lax.fori_loop(0, STRIPS, turn, 0, unroll=4)


def select_kernel(where_ref, aux_ref, q_ref, out_ref, meta_ref, hx_ref):
    def extract(i, _):
        g, j = i // OBS_CHUNKS, i % OBS_CHUNKS
        cell = aux_ref[pl.ds(g * 8 * AUX + LISTS + j, 8, stride=AUX), :].astype(jnp.int32)
        lanes = cell & (COLS - 1)
        line = cell >> 7
        rows = (line & (ROWS - 1)) * LEVELS + (line >> 2)
        sums = [jnp.zeros((8, COLS), F32) for _ in range(4)]
        for p in range(CELL_ROWS):
            src = q_ref[pl.ds(p + g * 8 * PITCH, 8, stride=PITCH), :]
            sums[p % 4] = jnp.where(rows == p, lane_gather(src, lanes), sums[p % 4])
        hx_ref[pl.ds(g * 64 + j, 8, stride=OBS_CHUNKS), :] = (sums[0] + sums[1]) + (sums[2] + sums[3])
        return 0

    lax.fori_loop(0, 2 * OBS_CHUNKS, extract, 0)

    def strip(a, _):
        for kb in range(PER_MEM):
            out_ref[pl.ds((kb * STRIPS + a) * SEND, COLS_HERE), :] = q_ref[
                pl.ds(pl.multiple_of(FIELD + a * CELL_ROWS + kb * COLS_HERE, 8), COLS_HERE), :
            ]
        sources = []
        for t in range(3):
            near = lax.rem(a + STRIPS - 1 + t, STRIPS) * OBS_CHUNKS
            for j in range(OBS_CHUNKS):
                sources.append(jnp.broadcast_to(hx_ref[pl.ds(near + j, 1), :], (8, COLS)))
        for g in range(PER_MEM // 2):
            slot = aux_ref[pl.ds(pl.multiple_of(a * AUX + g * 8, 8), 8), :].astype(jnp.int32)
            lanes = slot & (COLS - 1)
            chunk = slot >> 7
            found = lane_gather(sources[0], lanes)
            for j in range(1, META):
                found = jnp.where(chunk == j, lane_gather(sources[j], lanes), found)
            for i in range(2):
                kb = ((where_ref[1] >> 1) + ARRIVAL[g] & 7) * 2 + ((where_ref[1] & 1) ^ i)
                out_ref[pl.ds((kb * STRIPS + a) * SEND + COLS_HERE, SLOT_ROWS), :] = found[
                    i * SLOT_ROWS : (i + 1) * SLOT_ROWS
                ]
        return 0

    lax.fori_loop(0, STRIPS, strip, 0)

    meta_ref[...] = jnp.zeros_like(meta_ref)
    for t in range(3):
        strip = lax.rem(where_ref[0] + STRIPS - 1 + t, STRIPS)
        for which in range(3):
            meta_ref[pl.ds(t * 64 + which, 8, stride=8), :] = aux_ref[
                pl.ds(pl.multiple_of(strip * AUX + LISTS + which * 8, 8), 8), :
            ]


def parts(x):
    high = x.astype(BF16)
    return high, (x - high.astype(F32)).astype(BF16)


def product(a, b, dims=(((1,), (0,)), ((), ()))):
    def dot(x, y):
        return lax.dot_general(x, y, dims, preferred_element_type=F32)

    return dot(a[0], b[0]) + (dot(a[0], b[1]) + dot(a[1], b[0]))


def update_kernel(where_ref, count_ref, list_ref, meta_ref, in_ref, out_ref, it_ref, root_ref):
    members = 256
    row_id = lax.broadcasted_iota(jnp.int32, (members, members), 0)
    col_id = lax.broadcasted_iota(jnp.int32, (members, members), 1)
    diagonal = row_id == col_id
    slot_id = lax.broadcasted_iota(jnp.int32, (1, COLS), 1)

    def plus_identity(x, scale):
        return jnp.where(diagonal, x + scale, x)

    norms, drives = [], []
    for t in range(2):
        values, rhos, anomalies = [], [], []
        for h in range(2):
            slot = list_ref[pl.ds(2 * t + h, 1), :]
            wide = jnp.broadcast_to(slot, (8, COLS))
            lanes = wide & (COLS - 1)
            chunk = wide >> 7
            found = jnp.zeros((8, COLS), F32)
            for j in range(META):
                found = jnp.where(chunk == j, lane_gather(meta_ref[pl.ds(j * 8, 8), :], lanes), found)
            line = found[0:1].astype(jnp.int32)
            strip = where_ref[0] + STRIPS - 1 + (slot >> 10)
            strip = strip & (STRIPS - 1)
            place_x = (strip * ROWS + ((line >> 7) & (ROWS - 1))).astype(F32)
            place_y = (line & (COLS - 1)).astype(F32)
            centre_x = (where_ref[0] * 4).astype(F32) + 1.5
            centre_y = ((where_ref[1] * 2 + t) * 4).astype(F32) + 1.5
            dx = place_x - centre_x + 0.5 * HEIGHT
            dx = jnp.where(dx >= HEIGHT, dx - HEIGHT, dx)
            dx = jnp.where(dx < 0, dx + HEIGHT, dx) - 0.5 * HEIGHT
            dy = place_y - centre_y + 0.5 * COLS
            dy = jnp.where(dy >= COLS, dy - COLS, dy)
            dy = jnp.where(dy < 0, dy + COLS, dy) - 0.5 * COLS
            live = slot_id + h * COLS < count_ref[0, t]
            spread = found[2:3] * (1.0 + (dx * dx + dy * dy) / float(LOC * LOC))
            rho = jnp.where(live, 1.0 / spread, 0.0)
            obs = in_ref[pl.ds(COLS_HERE + 2 * t + h, members, stride=SEND), :]
            mean = jnp.sum(obs, axis=0, keepdims=True) * (1.0 / members)
            values.append(found[1:2] - mean)
            rhos.append(rho)
            anomalies.append(obs - mean)
        anomaly = jnp.concatenate(anomalies, axis=1)
        rho = jnp.concatenate(rhos, axis=1)
        innovation = jnp.concatenate(values, axis=1)
        drives.append(jnp.sum(anomaly * (rho * innovation), axis=1, keepdims=True))
        scaled = parts(anomaly * jnp.sqrt(rho))
        gram = product(scaled, scaled, (((1,), (1,)), ((), ())))
        gram = plus_identity(gram, (members - 1) / INFLATION)
        norm = jnp.sqrt(jnp.sum(jnp.sum(gram * gram, axis=1, keepdims=True), axis=0, keepdims=True))
        norms.append(norm)
        it = gram / norm
        factor = plus_identity(-0.5 * it, 1.5)
        root_ref[t] = factor
        it_ref[t] = product(parts(it), parts(factor))

    def iteration(_, c):
        roots = [parts(root_ref[t]) for t in range(2)]
        its = [parts(it_ref[t]) for t in range(2)]
        factors = [parts(plus_identity(-0.5 * product(roots[t], its[t]), 1.5)) for t in range(2)]
        for t in range(2):
            both = [jnp.concatenate([its[t][i], roots[t][i]], axis=0) for i in range(2)]
            both = product(both, factors[t])
            it_ref[t] = both[:members]
            root_ref[t] = both[members:]
        return c

    lax.fori_loop(0, NS_ITERS - 2, iteration, 0)

    roots = [parts(root_ref[t]) for t in range(2)]
    its = [parts(it_ref[t]) for t in range(2)]
    factors = [parts(plus_identity(-0.5 * product(roots[t], its[t]), 1.5)) for t in range(2)]
    fulls = [product(factors[t], roots[t]) for t in range(2)]
    for t in range(2):
        full = fulls[t]
        inner = jnp.sum(full * drives[t], axis=0, keepdims=True)
        shift = jnp.sum(full * inner, axis=1, keepdims=True) / norms[t]
        scale = jnp.sqrt((members - 1) / norms[t])
        root = parts(full * scale)
        for c in range(4 * t, 4 * t + 4):
            x = in_ref[pl.ds(c, members, stride=SEND), :]
            mean = jnp.sum(x, axis=0, keepdims=True) * (1.0 / members)
            x = x - mean
            moved = mean + jnp.sum(x * shift, axis=0, keepdims=True)
            out = product(root, parts(x)) + moved
            out_ref[:, c] = out.reshape(PER_MEM, PER_MEM, COLS)


def finish_kernel(in_ref, out_ref):
    def member(m, _):
        block = in_ref[pl.ds(m, COLS, stride=PER_MEM), :].T
        for r in range(ROWS):
            out_ref[pl.ds(m * CELL_ROWS + r, LEVELS, stride=ROWS), :] = block[r * LEVELS : (r + 1) * LEVELS]
        return 0

    lax.fori_loop(0, PER_MEM, member, 0, unroll=4)


PARAMS = pltpu.CompilerParams(vmem_limit_bytes=20 * 1024 * 1024)
SMEM = pl.BlockSpec(memory_space=pltpu.SMEM)
VMEM = pl.BlockSpec(memory_space=pltpu.VMEM)


def shards(prior, north, east, mix, obs_cell, obs_value, obs_var, tile_list, tile_count):
    dom, mem = lax.axis_index("dom"), lax.axis_index("mem")
    where = jnp.stack([dom, mem]).astype(jnp.int32)
    own = tile_list.reshape(SLOT_ROWS, COLS)
    def shifted(x, by):
        return lax.ppermute(x, "mem", [((i + by) % PER_MEM, i) for i in range(PER_MEM)])

    chip = jnp.concatenate(
        [own, lax.ppermute(own, "mem", [(i, i ^ 1) for i in range(PER_MEM)])], axis=0
    )
    ahead, behind = shifted(chip, 2), shifted(chip, -2)
    pieces = [
        chip, ahead, behind,
        shifted(jnp.concatenate([chip, ahead, behind], axis=0), 6),
        shifted(jnp.concatenate([chip, ahead], axis=0), -6),
    ]
    whole = lax.all_to_all(
        prior.reshape(PER_MEM, CELL_ROWS, COLS), "dom", split_axis=0, concat_axis=0, tiled=True
    )
    aux = pl.pallas_call(
        aux_kernel,
        compiler_params=PARAMS,
        name="aux",
        out_shape=jax.ShapeDtypeStruct((STRIPS * AUX, COLS), F32),
        in_specs=[VMEM] * 8,
        out_specs=VMEM,
    )(
        *pieces,
        obs_cell.reshape(OBS_CHUNKS, COLS),
        obs_value.reshape(OBS_CHUNKS, COLS),
        obs_var.reshape(OBS_CHUNKS, COLS),
    )
    every = lax.all_to_all(
        aux.reshape(STRIPS, AUX, COLS), "dom", split_axis=0, concat_axis=0, tiled=True
    )
    levels = pl.pallas_call(
        forecast_kernel,
        compiler_params=PARAMS,
        cost_estimate=pl.CostEstimate(flops=30_000_000, bytes_accessed=60_000_000, transcendentals=0),
        name="forecast",
        out_shape=jax.ShapeDtypeStruct((FIELD + STRIPS * CELL_ROWS, COLS), F32),
        in_specs=[SMEM, SMEM, SMEM, VMEM],
        out_specs=VMEM,
        scratch_shapes=[pltpu.VMEM((STRIPS * PITCH, COLS), F32)] * 2,
    )(north, east, mix, whole.reshape(STRIPS * CELL_ROWS, COLS))
    sent, near = pl.pallas_call(
        select_kernel,
        compiler_params=PARAMS,
        name="select",
        out_shape=(
            jax.ShapeDtypeStruct((PER_MEM * STRIPS * SEND, COLS), F32),
            jax.ShapeDtypeStruct((META * 8, COLS), F32),
        ),
        in_specs=[SMEM, VMEM, VMEM],
        out_specs=(VMEM, VMEM),
        scratch_shapes=[pltpu.VMEM((STRIPS * OBS_CHUNKS, COLS), F32)],
    )(where, every.reshape(STRIPS * AUX, COLS), levels)
    tiles = lax.all_to_all(
        sent.reshape(PER_MEM * STRIPS, SEND // 4, 4, COLS),
        ("mem", "dom"), split_axis=0, concat_axis=0, tiled=True,
    )
    updated = pl.pallas_call(
        update_kernel,
        compiler_params=PARAMS,
        name="update",
        out_shape=jax.ShapeDtypeStruct((PER_MEM, COLS_HERE, PER_MEM, COLS), F32),
        in_specs=[SMEM, SMEM, VMEM, VMEM, VMEM],
        out_specs=VMEM,
        scratch_shapes=[pltpu.VMEM((2, 256, 256), F32), pltpu.VMEM((2, 256, 256), F32)],
    )(where, tile_count, own, near, tiles.reshape(PER_MEM * STRIPS * SEND, COLS))
    back = lax.all_to_all(
        updated.reshape(PER_MEM, COLS_HERE * PER_MEM, COLS), "mem", split_axis=0, concat_axis=0, tiled=True
    )
    result = pl.pallas_call(
        finish_kernel,
        compiler_params=PARAMS,
        name="finish",
        out_shape=jax.ShapeDtypeStruct((PER_MEM * CELL_ROWS, COLS), F32),
        in_specs=[VMEM],
        out_specs=VMEM,
    )(back.reshape(PER_MEM * COLS_HERE * PER_MEM, COLS))
    return result.reshape(PER_MEM, LEVELS, ROWS, COLS)


def solution(mesh):
    placed = (
        P("mem", None, "dom", None),
        P(),
        P(),
        P(),
        P("dom"),
        P("dom"),
        P("dom"),
        P("dom", "mem", None),
        P("dom", "mem"),
    )
    return jax.shard_map(
        shards, mesh=mesh, in_specs=placed, out_specs=P("mem", None, "dom", None), check_vma=False
    )
```

```python
import jax
import jax.numpy as jnp
from jax import lax
from jax.experimental import pallas as pl
from jax.experimental.pallas import tpu as pltpu
from jax.sharding import PartitionSpec as P

LOC = 8
STEPS = 3
NS_ITERS = 5
INFLATION = 1.1

F32 = jnp.float32
BF16 = jnp.bfloat16
LEVELS = 32
ROWS = 4
COLS = 128
CELL_ROWS = LEVELS * ROWS
OBS_CHUNKS = 8
META = 3 * OBS_CHUNKS
SLOT_ROWS = 4
COLS_HERE = 8
SEND = COLS_HERE + SLOT_ROWS
PER_MEM = 16
STRIPS = 16
HEIGHT = STRIPS * ROWS
PITCH = CELL_ROWS + 8
FIELD = STRIPS * PITCH
LISTS = PER_MEM * SLOT_ROWS
AUX = LISTS + META


LANES = lax.GatherDimensionNumbers(
    offset_dims=(),
    collapsed_slice_dims=(1,),
    start_index_map=(1,),
    operand_batching_dims=(0,),
    start_indices_batching_dims=(0,),
)


def lane_gather(values, lanes):
    return lax.gather(
        values, lanes[..., None], LANES, (1, 1), mode=lax.GatherScatterMode.PROMISE_IN_BOUNDS
    )


ARRIVAL = (0, 1, 7, 3, 4, 2, 5, 6)


def aux_kernel(own_ref, l1_ref, l2_ref, l3_ref, l4_ref, cell_ref, value_ref, var_ref, out_ref):
    parts_in = [own_ref, l1_ref, l2_ref, l3_ref, l4_ref, cell_ref, value_ref, var_ref]
    for s in range(STRIPS):
        at = s * AUX
        for ref in parts_in:
            rows = ref.shape[0]
            out_ref[at : at + rows, :] = ref[...].astype(F32)
            at += rows


def forecast_kernel(north_ref, east_ref, mix_ref, in_ref, q_ref, t1_ref, t2_ref):
    def load(s, _):
        for r in range(ROWS):
            q_ref[pl.ds(pl.multiple_of(s * PITCH + r * LEVELS, 8), LEVELS), :] = in_ref[
                pl.ds(s * CELL_ROWS + r, LEVELS, stride=ROWS), :
            ]
        return 0

    lax.fori_loop(0, STRIPS, load, 0, unroll=4)

    def level_group(g, _):
        sub = lax.broadcasted_iota(jnp.int32, (8, COLS), 0)

        def spread(ref):
            value = jnp.full((8, COLS), ref[g * 8], F32)
            for i in range(1, 8):
                value = jnp.where(sub == i, ref[g * 8 + i], value)
            return value

        north, east, mix = spread(north_ref), spread(east_ref), spread(mix_ref)
        up, down = mix - 0.5 * north, mix + 0.5 * north
        right, left = mix - 0.5 * east, mix + 0.5 * east
        mid = -4.0 * mix

        def stage(src, dst, scale):
            a, b, c, d, e = up * scale, down * scale, right * scale, left * scale, mid * scale

            def at(ref, x):
                at_row = x // ROWS * PITCH + x % ROWS * LEVELS
                return ref.at[pl.ds(pl.multiple_of(at_row + g * 8, 8), 8), :]

            prev, cur = at(src, HEIGHT - 1)[...], at(src, 0)[...]
            first = cur
            for x in range(HEIGHT):
                nxt = first if x == HEIGHT - 1 else at(src, x + 1)[...]
                base = cur if src is q_ref else at(q_ref, x)[...]
                at(dst, x)[...] = (
                    base
                    + (a * nxt + b * prev)
                    + (c * pltpu.roll(cur, COLS - 1, 1) + d * pltpu.roll(cur, 1, 1))
                    + e * cur
                )
                prev, cur = cur, nxt

        def step(_, c):
            stage(q_ref, t1_ref, 1.0 / 3.0)
            stage(t1_ref, t2_ref, 0.5)
            stage(t2_ref, q_ref, 1.0)
            return c

        lax.fori_loop(0, STEPS, step, 0)
        return 0

    lax.fori_loop(0, LEVELS // 8, level_group, 0)

    def turn(s, _):
        q_ref[pl.ds(pl.multiple_of(FIELD + s * CELL_ROWS, 8), CELL_ROWS), :] = q_ref[
            pl.ds(pl.multiple_of(s * PITCH, 8), CELL_ROWS), :
        ].T
        return 0

    lax.fori_loop(0, STRIPS, turn, 0, unroll=4)


def select_kernel(where_ref, aux_ref, q_ref, out_ref, meta_ref, hx_ref):
    sub = lax.broadcasted_iota(jnp.int32, (COLS, 2 * COLS), 0)

    def extract(s):
        s = lax.rem(s, STRIPS)
        cell = aux_ref[pl.ds(pl.multiple_of(s * AUX + LISTS, 8), 8), :].astype(jnp.int32)
        lanes = cell & (COLS - 1)
        line = cell >> 7
        rows = (line & (ROWS - 1)) * LEVELS + (line >> 2)
        block = q_ref[pl.ds(pl.multiple_of(FIELD + s * CELL_ROWS, 8), CELL_ROWS), :]
        high = block.astype(BF16)
        rest = block - high.astype(F32)
        middle = rest.astype(BF16)
        low = (rest - middle.astype(F32)).astype(BF16)
        block = jnp.concatenate([high, middle, low], axis=1)
        found = []
        for j in range(0, OBS_CHUNKS, 2):
            row = jnp.concatenate([rows[j : j + 1], rows[j + 1 : j + 2]], axis=1)
            lane = jnp.concatenate([lanes[j : j + 1], lanes[j + 1 : j + 2]], axis=1)
            pick = jnp.where(sub == row, 1.0, 0.0).astype(BF16)
            picked = jnp.dot(
                block, jnp.concatenate([pick, pick, pick], axis=0), preferred_element_type=F32
            )
            picked = jnp.sum(jnp.where(sub == lane, picked, 0.0), axis=0, keepdims=True)
            found += [picked[:, :COLS], picked[:, COLS:]]
        for j in range(OBS_CHUNKS):
            hx_ref[pl.ds(s * OBS_CHUNKS + j, 1), :] = found[j]

    def first(i, _):
        extract(i + STRIPS - 1)
        return 0

    lax.fori_loop(0, 3, first, 0)

    def strip(a, _):
        for kb in range(PER_MEM):
            out_ref[pl.ds((kb * STRIPS + a) * SEND, COLS_HERE), :] = q_ref[
                pl.ds(pl.multiple_of(FIELD + a * CELL_ROWS + kb * COLS_HERE, 8), COLS_HERE), :
            ]
        sources = []
        for t in range(3):
            near = lax.rem(a + STRIPS - 1 + t, STRIPS) * OBS_CHUNKS
            for j in range(OBS_CHUNKS):
                sources.append(jnp.broadcast_to(hx_ref[pl.ds(near + j, 1), :], (8, COLS)))
        for g in range(PER_MEM // 2):
            slot = aux_ref[pl.ds(pl.multiple_of(a * AUX + g * 8, 8), 8), :].astype(jnp.int32)
            lanes = slot & (COLS - 1)
            chunk = slot >> 7
            found = lane_gather(sources[0], lanes)
            for j in range(1, META):
                found = jnp.where(chunk == j, lane_gather(sources[j], lanes), found)
            for i in range(2):
                kb = ((where_ref[1] >> 1) + ARRIVAL[g] & 7) * 2 + ((where_ref[1] & 1) ^ i)
                out_ref[pl.ds((kb * STRIPS + a) * SEND + COLS_HERE, SLOT_ROWS), :] = found[
                    i * SLOT_ROWS : (i + 1) * SLOT_ROWS
                ]
        extract(a + 2)
        return 0

    lax.fori_loop(0, STRIPS, strip, 0)

    meta_ref[...] = jnp.zeros_like(meta_ref)
    for t in range(3):
        strip = lax.rem(where_ref[0] + STRIPS - 1 + t, STRIPS)
        for which in range(3):
            meta_ref[pl.ds(t * 64 + which, 8, stride=8), :] = aux_ref[
                pl.ds(pl.multiple_of(strip * AUX + LISTS + which * 8, 8), 8), :
            ]


def parts(x):
    high = x.astype(BF16)
    return high, (x - high.astype(F32)).astype(BF16)


def product(a, b, dims=(((1,), (0,)), ((), ()))):
    def dot(x, y):
        return lax.dot_general(x, y, dims, preferred_element_type=F32)

    return dot(a[0], b[0]) + (dot(a[0], b[1]) + dot(a[1], b[0]))


def update_kernel(where_ref, count_ref, list_ref, meta_ref, in_ref, out_ref, it_ref, root_ref):
    members = 256
    row_id = lax.broadcasted_iota(jnp.int32, (members, members), 0)
    col_id = lax.broadcasted_iota(jnp.int32, (members, members), 1)
    diagonal = row_id == col_id
    slot_id = lax.broadcasted_iota(jnp.int32, (1, COLS), 1)

    def plus_identity(x, scale):
        return jnp.where(diagonal, x + scale, x)

    norms, drives = [], []
    for t in range(2):
        values, rhos, anomalies = [], [], []
        for h in range(2):
            slot = list_ref[pl.ds(2 * t + h, 1), :]
            wide = jnp.broadcast_to(slot, (8, COLS))
            lanes = wide & (COLS - 1)
            chunk = wide >> 7
            found = jnp.zeros((8, COLS), F32)
            for j in range(META):
                found = jnp.where(chunk == j, lane_gather(meta_ref[pl.ds(j * 8, 8), :], lanes), found)
            line = found[0:1].astype(jnp.int32)
            strip = where_ref[0] + STRIPS - 1 + (slot >> 10)
            strip = strip & (STRIPS - 1)
            place_x = (strip * ROWS + ((line >> 7) & (ROWS - 1))).astype(F32)
            place_y = (line & (COLS - 1)).astype(F32)
            centre_x = (where_ref[0] * 4).astype(F32) + 1.5
            centre_y = ((where_ref[1] * 2 + t) * 4).astype(F32) + 1.5
            dx = place_x - centre_x + 0.5 * HEIGHT
            dx = jnp.where(dx >= HEIGHT, dx - HEIGHT, dx)
            dx = jnp.where(dx < 0, dx + HEIGHT, dx) - 0.5 * HEIGHT
            dy = place_y - centre_y + 0.5 * COLS
            dy = jnp.where(dy >= COLS, dy - COLS, dy)
            dy = jnp.where(dy < 0, dy + COLS, dy) - 0.5 * COLS
            live = slot_id + h * COLS < count_ref[0, t]
            spread = found[2:3] * (1.0 + (dx * dx + dy * dy) / float(LOC * LOC))
            rho = jnp.where(live, 1.0 / spread, 0.0)
            obs = in_ref[pl.ds(COLS_HERE + 2 * t + h, members, stride=SEND), :]
            mean = jnp.sum(obs, axis=0, keepdims=True) * (1.0 / members)
            values.append(found[1:2] - mean)
            rhos.append(rho)
            anomalies.append(obs - mean)
        anomaly = jnp.concatenate(anomalies, axis=1)
        rho = jnp.concatenate(rhos, axis=1)
        innovation = jnp.concatenate(values, axis=1)
        drives.append(jnp.sum(anomaly * (rho * innovation), axis=1, keepdims=True))
        scaled = parts(anomaly * jnp.sqrt(rho))
        gram = product(scaled, scaled, (((1,), (1,)), ((), ())))
        gram = plus_identity(gram, (members - 1) / INFLATION)
        norm = jnp.sqrt(jnp.sum(jnp.sum(gram * gram, axis=1, keepdims=True), axis=0, keepdims=True))
        norms.append(norm)
        it = gram / norm
        factor = plus_identity(-0.5 * it, 1.5)
        root_ref[t] = factor
        it_ref[t] = product(parts(it), parts(factor))

    def iteration(_, c):
        roots = [parts(root_ref[t]) for t in range(2)]
        its = [parts(it_ref[t]) for t in range(2)]
        factors = [parts(plus_identity(-0.5 * product(roots[t], its[t]), 1.5)) for t in range(2)]
        for t in range(2):
            both = [jnp.concatenate([its[t][i], roots[t][i]], axis=0) for i in range(2)]
            both = product(both, factors[t])
            it_ref[t] = both[:members]
            root_ref[t] = both[members:]
        return c

    lax.fori_loop(0, NS_ITERS - 2, iteration, 0)

    roots = [parts(root_ref[t]) for t in range(2)]
    its = [parts(it_ref[t]) for t in range(2)]
    factors = [parts(plus_identity(-0.5 * product(roots[t], its[t]), 1.5)) for t in range(2)]
    fulls = [product(factors[t], roots[t]) for t in range(2)]
    for t in range(2):
        full = fulls[t]
        inner = jnp.sum(full * drives[t], axis=0, keepdims=True)
        shift = jnp.sum(full * inner, axis=1, keepdims=True) / norms[t]
        scale = jnp.sqrt((members - 1) / norms[t])
        root = parts(full * scale)
        for c in range(4 * t, 4 * t + 4, 2):
            x = jnp.concatenate(
                [in_ref[pl.ds(c + i, members, stride=SEND), :] for i in range(2)], axis=1
            )
            mean = jnp.sum(x, axis=0, keepdims=True) * (1.0 / members)
            x = x - mean
            moved = mean + jnp.sum(x * shift, axis=0, keepdims=True)
            out = product(root, parts(x)) + moved
            for i in range(2):
                out_ref[:, c + i] = out[:, i * COLS : (i + 1) * COLS].reshape(PER_MEM, PER_MEM, COLS)


def finish_kernel(in_ref, out_ref):
    def member(m, _):
        block = in_ref[pl.ds(m, COLS, stride=PER_MEM), :].T
        for r in range(ROWS):
            out_ref[pl.ds(m * CELL_ROWS + r, LEVELS, stride=ROWS), :] = block[r * LEVELS : (r + 1) * LEVELS]
        return 0

    lax.fori_loop(0, PER_MEM, member, 0, unroll=4)


PARAMS = pltpu.CompilerParams(vmem_limit_bytes=20 * 1024 * 1024)
SMEM = pl.BlockSpec(memory_space=pltpu.SMEM)
VMEM = pl.BlockSpec(memory_space=pltpu.VMEM)


def shards(prior, north, east, mix, obs_cell, obs_value, obs_var, tile_list, tile_count):
    dom, mem = lax.axis_index("dom"), lax.axis_index("mem")
    where = jnp.stack([dom, mem]).astype(jnp.int32)
    own = tile_list.reshape(SLOT_ROWS, COLS)
    def shifted(x, by):
        return lax.ppermute(x, "mem", [((i + by) % PER_MEM, i) for i in range(PER_MEM)])

    chip = jnp.concatenate(
        [own, lax.ppermute(own, "mem", [(i, i ^ 1) for i in range(PER_MEM)])], axis=0
    )
    ahead, behind = shifted(chip, 2), shifted(chip, -2)
    pieces = [
        chip, ahead, behind,
        shifted(jnp.concatenate([chip, ahead, behind], axis=0), 6),
        shifted(jnp.concatenate([chip, ahead], axis=0), -6),
    ]
    whole = lax.all_to_all(
        prior.reshape(PER_MEM, CELL_ROWS, COLS), "dom", split_axis=0, concat_axis=0, tiled=True
    )
    aux = pl.pallas_call(
        aux_kernel,
        compiler_params=PARAMS,
        name="aux",
        out_shape=jax.ShapeDtypeStruct((STRIPS * AUX, COLS), F32),
        in_specs=[VMEM] * 8,
        out_specs=VMEM,
    )(
        *pieces,
        obs_cell.reshape(OBS_CHUNKS, COLS),
        obs_value.reshape(OBS_CHUNKS, COLS),
        obs_var.reshape(OBS_CHUNKS, COLS),
    )
    every = lax.all_to_all(
        aux.reshape(STRIPS, AUX, COLS), "dom", split_axis=0, concat_axis=0, tiled=True
    )
    levels = pl.pallas_call(
        forecast_kernel,
        compiler_params=PARAMS,
        cost_estimate=pl.CostEstimate(flops=30_000_000, bytes_accessed=60_000_000, transcendentals=0),
        name="forecast",
        out_shape=jax.ShapeDtypeStruct((FIELD + STRIPS * CELL_ROWS, COLS), F32),
        in_specs=[SMEM, SMEM, SMEM, VMEM],
        out_specs=VMEM,
        scratch_shapes=[pltpu.VMEM((STRIPS * PITCH, COLS), F32)] * 2,
    )(north, east, mix, whole.reshape(STRIPS * CELL_ROWS, COLS))
    sent, near = pl.pallas_call(
        select_kernel,
        compiler_params=PARAMS,
        name="select",
        out_shape=(
            jax.ShapeDtypeStruct((PER_MEM * STRIPS * SEND, COLS), F32),
            jax.ShapeDtypeStruct((META * 8, COLS), F32),
        ),
        in_specs=[SMEM, VMEM, VMEM],
        out_specs=(VMEM, VMEM),
        scratch_shapes=[pltpu.VMEM((STRIPS * OBS_CHUNKS, COLS), F32)],
    )(where, every.reshape(STRIPS * AUX, COLS), levels)
    tiles = lax.all_to_all(
        sent.reshape(PER_MEM * STRIPS, SEND // 4, 4, COLS),
        ("mem", "dom"), split_axis=0, concat_axis=0, tiled=True,
    )
    updated = pl.pallas_call(
        update_kernel,
        compiler_params=PARAMS,
        name="update",
        out_shape=jax.ShapeDtypeStruct((PER_MEM, COLS_HERE, PER_MEM, COLS), F32),
        in_specs=[SMEM, SMEM, VMEM, VMEM, VMEM],
        out_specs=VMEM,
        scratch_shapes=[pltpu.VMEM((2, 256, 256), F32), pltpu.VMEM((2, 256, 256), F32)],
    )(where, tile_count, own, near, tiles.reshape(PER_MEM * STRIPS * SEND, COLS))
    back = lax.all_to_all(
        updated.reshape(PER_MEM, COLS_HERE * PER_MEM, COLS), "mem", split_axis=0, concat_axis=0, tiled=True
    )
    result = pl.pallas_call(
        finish_kernel,
        compiler_params=PARAMS,
        name="finish",
        out_shape=jax.ShapeDtypeStruct((PER_MEM * CELL_ROWS, COLS), F32),
        in_specs=[VMEM],
        out_specs=VMEM,
    )(back.reshape(PER_MEM * COLS_HERE * PER_MEM, COLS))
    return result.reshape(PER_MEM, LEVELS, ROWS, COLS)


def solution(mesh):
    placed = (
        P("mem", None, "dom", None),
        P(),
        P(),
        P(),
        P("dom"),
        P("dom"),
        P("dom"),
        P("dom", "mem", None),
        P("dom", "mem"),
    )
    return jax.shard_map(
        shards, mesh=mesh, in_specs=placed, out_specs=P("mem", None, "dom", None), check_vma=False
    )
```

```python
import jax
import jax.numpy as jnp
from jax import lax
from jax.experimental import pallas as pl
from jax.experimental.pallas import tpu as pltpu
from jax.sharding import PartitionSpec as P

LOC = 8
STEPS = 3
NS_ITERS = 5
INFLATION = 1.1

F32 = jnp.float32
BF16 = jnp.bfloat16
LEVELS = 32
ROWS = 4
COLS = 128
CELL_ROWS = LEVELS * ROWS
OBS_CHUNKS = 8
META = 3 * OBS_CHUNKS
SLOT_ROWS = 4
COLS_HERE = 8
SEND = COLS_HERE + SLOT_ROWS
PER_MEM = 16
STRIPS = 16
HEIGHT = STRIPS * ROWS
PITCH = CELL_ROWS + 8
FIELD = STRIPS * PITCH
LISTS = PER_MEM * SLOT_ROWS
AUX = LISTS + META


LANES = lax.GatherDimensionNumbers(
    offset_dims=(),
    collapsed_slice_dims=(1,),
    start_index_map=(1,),
    operand_batching_dims=(0,),
    start_indices_batching_dims=(0,),
)


def lane_gather(values, lanes):
    return lax.gather(
        values, lanes[..., None], LANES, (1, 1), mode=lax.GatherScatterMode.PROMISE_IN_BOUNDS
    )


ARRIVAL = (0, 1, 7, 3, 4, 2, 5, 6)


def aux_kernel(own_ref, l1_ref, l2_ref, l3_ref, l4_ref, cell_ref, value_ref, var_ref, out_ref):
    parts_in = [own_ref, l1_ref, l2_ref, l3_ref, l4_ref, cell_ref, value_ref, var_ref]
    for s in range(STRIPS):
        at = s * AUX
        for ref in parts_in:
            rows = ref.shape[0]
            out_ref[at : at + rows, :] = ref[...].astype(F32)
            at += rows


def forecast_kernel(north_ref, east_ref, mix_ref, in_ref, q_ref, t1_ref, t2_ref):
    def load(s, _):
        for r in range(ROWS):
            q_ref[pl.ds(pl.multiple_of(s * PITCH + r * LEVELS, 8), LEVELS), :] = in_ref[
                pl.ds(s * CELL_ROWS + r, LEVELS, stride=ROWS), :
            ]
        return 0

    lax.fori_loop(0, STRIPS, load, 0, unroll=4)

    def level_group(g, _):
        sub = lax.broadcasted_iota(jnp.int32, (8, COLS), 0)

        def spread(ref):
            value = jnp.full((8, COLS), ref[g * 8], F32)
            for i in range(1, 8):
                value = jnp.where(sub == i, ref[g * 8 + i], value)
            return value

        north, east, mix = spread(north_ref), spread(east_ref), spread(mix_ref)
        up, down = mix - 0.5 * north, mix + 0.5 * north
        right, left = mix - 0.5 * east, mix + 0.5 * east
        mid = -4.0 * mix

        def stage(src, dst, scale):
            a, b, c, d, e = up * scale, down * scale, right * scale, left * scale, mid * scale

            def at(ref, x):
                at_row = x // ROWS * PITCH + x % ROWS * LEVELS
                return ref.at[pl.ds(pl.multiple_of(at_row + g * 8, 8), 8), :]

            prev, cur = at(src, HEIGHT - 1)[...], at(src, 0)[...]
            first = cur
            for x in range(HEIGHT):
                nxt = first if x == HEIGHT - 1 else at(src, x + 1)[...]
                base = cur if src is q_ref else at(q_ref, x)[...]
                at(dst, x)[...] = (
                    base
                    + (a * nxt + b * prev)
                    + (c * pltpu.roll(cur, COLS - 1, 1) + d * pltpu.roll(cur, 1, 1))
                    + e * cur
                )
                prev, cur = cur, nxt

        def step(_, c):
            stage(q_ref, t1_ref, 1.0 / 3.0)
            stage(t1_ref, t2_ref, 0.5)
            stage(t2_ref, q_ref, 1.0)
            return c

        lax.fori_loop(0, STEPS, step, 0)
        return 0

    lax.fori_loop(0, LEVELS // 8, level_group, 0)

    def turn(s, _):
        q_ref[pl.ds(pl.multiple_of(FIELD + s * CELL_ROWS, 8), CELL_ROWS), :] = q_ref[
            pl.ds(pl.multiple_of(s * PITCH, 8), CELL_ROWS), :
        ].T
        return 0

    lax.fori_loop(0, STRIPS, turn, 0, unroll=4)


def select_kernel(where_ref, aux_ref, q_ref, out_ref, meta_ref, hx_ref):
    sub = lax.broadcasted_iota(jnp.int32, (COLS, 2 * COLS), 0)

    def extract(s):
        s = lax.rem(s, STRIPS)
        cell = aux_ref[pl.ds(pl.multiple_of(s * AUX + LISTS, 8), 8), :].astype(jnp.int32)
        lanes = cell & (COLS - 1)
        line = cell >> 7
        rows = (line & (ROWS - 1)) * LEVELS + (line >> 2)
        block = q_ref[pl.ds(pl.multiple_of(FIELD + s * CELL_ROWS, 8), CELL_ROWS), :]
        high = block.astype(BF16)
        rest = block - high.astype(F32)
        middle = rest.astype(BF16)
        low = (rest - middle.astype(F32)).astype(BF16)
        block = jnp.concatenate([high, middle, low], axis=1)
        found = []
        for j in range(0, OBS_CHUNKS, 2):
            row = jnp.concatenate([rows[j : j + 1], rows[j + 1 : j + 2]], axis=1)
            lane = jnp.concatenate([lanes[j : j + 1], lanes[j + 1 : j + 2]], axis=1)
            pick = jnp.where(sub == row, 1.0, 0.0).astype(BF16)
            picked = jnp.dot(
                block, jnp.concatenate([pick, pick, pick], axis=0), preferred_element_type=F32
            )
            picked = jnp.sum(jnp.where(sub == lane, picked, 0.0), axis=0, keepdims=True)
            found += [picked[:, :COLS], picked[:, COLS:]]
        for j in range(OBS_CHUNKS):
            hx_ref[pl.ds(s * OBS_CHUNKS + j, 1), :] = found[j]

    def first(i, _):
        extract(i + STRIPS - 1)
        return 0

    lax.fori_loop(0, 3, first, 0, unroll=3)

    def strip(a, _):
        for kb in range(PER_MEM):
            out_ref[pl.ds((kb * STRIPS + a) * SEND, COLS_HERE), :] = q_ref[
                pl.ds(pl.multiple_of(FIELD + a * CELL_ROWS + kb * COLS_HERE, 8), COLS_HERE), :
            ]
        sources = []
        for t in range(3):
            near = lax.rem(a + STRIPS - 1 + t, STRIPS) * OBS_CHUNKS
            for j in range(OBS_CHUNKS):
                sources.append(jnp.broadcast_to(hx_ref[pl.ds(near + j, 1), :], (8, COLS)))
        for g in range(PER_MEM // 2):
            slot = aux_ref[pl.ds(pl.multiple_of(a * AUX + g * 8, 8), 8), :].astype(jnp.int32)
            lanes = slot & (COLS - 1)
            chunk = slot >> 7
            found = lane_gather(sources[0], lanes)
            for j in range(1, META):
                found = jnp.where(chunk == j, lane_gather(sources[j], lanes), found)
            for i in range(2):
                kb = ((where_ref[1] >> 1) + ARRIVAL[g] & 7) * 2 + ((where_ref[1] & 1) ^ i)
                out_ref[pl.ds((kb * STRIPS + a) * SEND + COLS_HERE, SLOT_ROWS), :] = found[
                    i * SLOT_ROWS : (i + 1) * SLOT_ROWS
                ]
        extract(a + 2)
        return 0

    lax.fori_loop(0, STRIPS, strip, 0)

    meta_ref[...] = jnp.zeros_like(meta_ref)
    for t in range(3):
        strip = lax.rem(where_ref[0] + STRIPS - 1 + t, STRIPS)
        for which in range(3):
            meta_ref[pl.ds(t * 64 + which, 8, stride=8), :] = aux_ref[
                pl.ds(pl.multiple_of(strip * AUX + LISTS + which * 8, 8), 8), :
            ]


def parts(x):
    high = x.astype(BF16)
    return high, (x - high.astype(F32)).astype(BF16)


def product(a, b, dims=(((1,), (0,)), ((), ()))):
    def dot(x, y):
        return lax.dot_general(x, y, dims, preferred_element_type=F32)

    return dot(a[0], b[0]) + (dot(a[0], b[1]) + dot(a[1], b[0]))


def update_kernel(where_ref, count_ref, list_ref, meta_ref, in_ref, out_ref, it_ref, root_ref):
    members = 256
    row_id = lax.broadcasted_iota(jnp.int32, (members, members), 0)
    col_id = lax.broadcasted_iota(jnp.int32, (members, members), 1)
    diagonal = row_id == col_id
    slot_id = lax.broadcasted_iota(jnp.int32, (1, COLS), 1)

    def plus_identity(x, scale):
        return jnp.where(diagonal, x + scale, x)

    drives, scales = [], []
    for t in range(2):
        values, rhos, anomalies = [], [], []
        for h in range(2):
            slot = list_ref[pl.ds(2 * t + h, 1), :]
            wide = jnp.broadcast_to(slot, (8, COLS))
            lanes = wide & (COLS - 1)
            chunk = wide >> 7
            found = jnp.zeros((8, COLS), F32)
            for j in range(META):
                found = jnp.where(chunk == j, lane_gather(meta_ref[pl.ds(j * 8, 8), :], lanes), found)
            line = found[0:1].astype(jnp.int32)
            strip = where_ref[0] + STRIPS - 1 + (slot >> 10)
            strip = strip & (STRIPS - 1)
            place_x = (strip * ROWS + ((line >> 7) & (ROWS - 1))).astype(F32)
            place_y = (line & (COLS - 1)).astype(F32)
            centre_x = (where_ref[0] * 4).astype(F32) + 1.5
            centre_y = ((where_ref[1] * 2 + t) * 4).astype(F32) + 1.5
            dx = place_x - centre_x + 0.5 * HEIGHT
            dx = jnp.where(dx >= HEIGHT, dx - HEIGHT, dx)
            dx = jnp.where(dx < 0, dx + HEIGHT, dx) - 0.5 * HEIGHT
            dy = place_y - centre_y + 0.5 * COLS
            dy = jnp.where(dy >= COLS, dy - COLS, dy)
            dy = jnp.where(dy < 0, dy + COLS, dy) - 0.5 * COLS
            live = slot_id + h * COLS < count_ref[0, t]
            spread = found[2:3] * (1.0 + (dx * dx + dy * dy) / float(LOC * LOC))
            rho = jnp.where(live, 1.0 / spread, 0.0)
            obs = in_ref[pl.ds(COLS_HERE + 2 * t + h, members, stride=SEND), :]
            mean = jnp.sum(obs, axis=0, keepdims=True) * (1.0 / members)
            values.append(found[1:2] - mean)
            rhos.append(rho)
            anomalies.append(obs - mean)
        anomaly = jnp.concatenate(anomalies, axis=1)
        rho = jnp.concatenate(rhos, axis=1)
        innovation = jnp.concatenate(values, axis=1)
        drives.append(jnp.sum(anomaly * (rho * innovation), axis=1, keepdims=True))
        scales.append(parts(anomaly * jnp.sqrt(rho)))
    grams = [
        plus_identity(product(x, x, (((1,), (1,)), ((), ()))), (members - 1) / INFLATION) for x in scales
    ]
    norms = [
        jnp.sqrt(jnp.sum(jnp.sum(x * x, axis=0, keepdims=True), axis=1, keepdims=True)) for x in grams
    ]
    its = [gram / norm for gram, norm in zip(grams, norms)]
    factors = [plus_identity(-0.5 * it, 1.5) for it in its]
    for t in range(2):
        root_ref[t] = factors[t]
        it_ref[t] = product(parts(its[t]), parts(factors[t]))

    def iteration(_, c):
        roots = [parts(root_ref[t]) for t in range(2)]
        its = [parts(it_ref[t]) for t in range(2)]
        factors = [parts(plus_identity(-0.5 * product(roots[t], its[t]), 1.5)) for t in range(2)]
        for t in range(2):
            both = [jnp.concatenate([its[t][i], roots[t][i]], axis=0) for i in range(2)]
            both = product(both, factors[t])
            it_ref[t] = both[:members]
            root_ref[t] = both[members:]
        return c

    lax.fori_loop(0, NS_ITERS - 2, iteration, 0)

    roots = [parts(root_ref[t]) for t in range(2)]
    its = [parts(it_ref[t]) for t in range(2)]
    factors = [parts(plus_identity(-0.5 * product(roots[t], its[t]), 1.5)) for t in range(2)]
    fulls = [product(factors[t], roots[t]) for t in range(2)]
    for t in range(2):
        full = fulls[t]
        inner = jnp.sum(full * drives[t], axis=0, keepdims=True)
        shift = jnp.sum(full * inner, axis=1, keepdims=True) / norms[t]
        scale = jnp.sqrt((members - 1) / norms[t])
        root = parts(full * scale)
        for c in range(4 * t, 4 * t + 4, 2):
            x = jnp.concatenate(
                [in_ref[pl.ds(c + i, members, stride=SEND), :] for i in range(2)], axis=1
            )
            mean = jnp.sum(x, axis=0, keepdims=True) * (1.0 / members)
            x = x - mean
            moved = mean + jnp.sum(x * shift, axis=0, keepdims=True)
            out = product(root, parts(x)) + moved
            for i in range(2):
                out_ref[:, c + i] = out[:, i * COLS : (i + 1) * COLS].reshape(PER_MEM, PER_MEM, COLS)


def finish_kernel(in_ref, out_ref, turned_ref, sems):
    group = 4

    def copy(g):
        rows = pl.ds(g * group * CELL_ROWS, group * CELL_ROWS)
        return pltpu.make_async_copy(turned_ref.at[rows, :], out_ref.at[rows, :], sems.at[g])

    for g in range(PER_MEM // group):
        for m in range(g * group, (g + 1) * group):
            block = in_ref[pl.ds(m, COLS, stride=PER_MEM), :].T
            for r in range(ROWS):
                turned_ref[pl.ds(m * CELL_ROWS + r, LEVELS, stride=ROWS), :] = block[
                    r * LEVELS : (r + 1) * LEVELS
                ]
        copy(g).start()
    for g in range(PER_MEM // group):
        copy(g).wait()


PARAMS = pltpu.CompilerParams(vmem_limit_bytes=20 * 1024 * 1024)
SMEM = pl.BlockSpec(memory_space=pltpu.SMEM)
VMEM = pl.BlockSpec(memory_space=pltpu.VMEM)


def shards(prior, north, east, mix, obs_cell, obs_value, obs_var, tile_list, tile_count):
    dom, mem = lax.axis_index("dom"), lax.axis_index("mem")
    where = jnp.stack([dom, mem]).astype(jnp.int32)
    own = tile_list.reshape(SLOT_ROWS, COLS)
    def shifted(x, by):
        return lax.ppermute(x, "mem", [((i + by) % PER_MEM, i) for i in range(PER_MEM)])

    chip = jnp.concatenate(
        [own, lax.ppermute(own, "mem", [(i, i ^ 1) for i in range(PER_MEM)])], axis=0
    )
    ahead, behind = shifted(chip, 2), shifted(chip, -2)
    pieces = [
        chip, ahead, behind,
        shifted(jnp.concatenate([chip, ahead, behind], axis=0), 6),
        shifted(jnp.concatenate([chip, ahead], axis=0), -6),
    ]
    whole = lax.all_to_all(
        prior.reshape(PER_MEM, CELL_ROWS, COLS), "dom", split_axis=0, concat_axis=0, tiled=True
    )
    aux = pl.pallas_call(
        aux_kernel,
        compiler_params=PARAMS,
        name="aux",
        out_shape=jax.ShapeDtypeStruct((STRIPS * AUX, COLS), F32),
        in_specs=[VMEM] * 8,
        out_specs=VMEM,
    )(
        *pieces,
        obs_cell.reshape(OBS_CHUNKS, COLS),
        obs_value.reshape(OBS_CHUNKS, COLS),
        obs_var.reshape(OBS_CHUNKS, COLS),
    )
    every = lax.all_to_all(
        aux.reshape(STRIPS, AUX, COLS), "dom", split_axis=0, concat_axis=0, tiled=True
    )
    levels = pl.pallas_call(
        forecast_kernel,
        compiler_params=PARAMS,
        cost_estimate=pl.CostEstimate(flops=30_000_000, bytes_accessed=60_000_000, transcendentals=0),
        name="forecast",
        out_shape=jax.ShapeDtypeStruct((FIELD + STRIPS * CELL_ROWS, COLS), F32),
        in_specs=[SMEM, SMEM, SMEM, VMEM],
        out_specs=VMEM,
        scratch_shapes=[pltpu.VMEM((STRIPS * PITCH, COLS), F32)] * 2,
    )(north, east, mix, whole.reshape(STRIPS * CELL_ROWS, COLS))
    sent, near = pl.pallas_call(
        select_kernel,
        compiler_params=PARAMS,
        name="select",
        out_shape=(
            jax.ShapeDtypeStruct((PER_MEM * STRIPS * SEND, COLS), F32),
            jax.ShapeDtypeStruct((META * 8, COLS), F32),
        ),
        in_specs=[SMEM, VMEM, VMEM],
        out_specs=(VMEM, VMEM),
        scratch_shapes=[pltpu.VMEM((STRIPS * OBS_CHUNKS, COLS), F32)],
    )(where, every.reshape(STRIPS * AUX, COLS), levels)
    tiles = lax.all_to_all(
        sent.reshape(PER_MEM * STRIPS, SEND // 4, 4, COLS),
        ("mem", "dom"), split_axis=0, concat_axis=0, tiled=True,
    )
    updated = pl.pallas_call(
        update_kernel,
        compiler_params=PARAMS,
        name="update",
        out_shape=jax.ShapeDtypeStruct((PER_MEM, COLS_HERE, PER_MEM, COLS), F32),
        in_specs=[SMEM, SMEM, VMEM, VMEM, VMEM],
        out_specs=VMEM,
        scratch_shapes=[pltpu.VMEM((2, 256, 256), F32), pltpu.VMEM((2, 256, 256), F32)],
    )(where, tile_count, own, near, tiles.reshape(PER_MEM * STRIPS * SEND, COLS))
    back = lax.all_to_all(
        updated.reshape(PER_MEM, COLS_HERE * PER_MEM, COLS), "mem", split_axis=0, concat_axis=0, tiled=True
    )
    result = pl.pallas_call(
        finish_kernel,
        compiler_params=PARAMS,
        name="finish",
        out_shape=jax.ShapeDtypeStruct((PER_MEM * CELL_ROWS, COLS), F32),
        in_specs=[VMEM],
        out_specs=pl.BlockSpec(memory_space=pl.ANY),
        scratch_shapes=[
            pltpu.VMEM((PER_MEM * CELL_ROWS, COLS), F32),
            pltpu.SemaphoreType.DMA((4,)),
        ],
    )(back.reshape(PER_MEM * COLS_HERE * PER_MEM, COLS))
    return result.reshape(PER_MEM, LEVELS, ROWS, COLS)


def solution(mesh):
    placed = (
        P("mem", None, "dom", None),
        P(),
        P(),
        P(),
        P("dom"),
        P("dom"),
        P("dom"),
        P("dom", "mem", None),
        P("dom", "mem"),
    )
    return jax.shard_map(
        shards, mesh=mesh, in_specs=placed, out_specs=P("mem", None, "dom", None), check_vma=False
    )
```

```python
import jax
import jax.numpy as jnp
from jax import lax
from jax.experimental import pallas as pl
from jax.experimental.pallas import tpu as pltpu
from jax.sharding import PartitionSpec as P

LOC = 8
STEPS = 3
NS_ITERS = 5
INFLATION = 1.1

F32 = jnp.float32
BF16 = jnp.bfloat16
LEVELS = 32
ROWS = 4
COLS = 128
CELL_ROWS = LEVELS * ROWS
OBS_CHUNKS = 8
META = 3 * OBS_CHUNKS
SLOT_ROWS = 4
COLS_HERE = 8
SEND = COLS_HERE + SLOT_ROWS
PER_MEM = 16
STRIPS = 16
HEIGHT = STRIPS * ROWS
PITCH = CELL_ROWS + 8
FIELD = STRIPS * PITCH
LISTS = PER_MEM * SLOT_ROWS
AUX = LISTS + OBS_CHUNKS


LANES = lax.GatherDimensionNumbers(
    offset_dims=(),
    collapsed_slice_dims=(1,),
    start_index_map=(1,),
    operand_batching_dims=(0,),
    start_indices_batching_dims=(0,),
)


def lane_gather(values, lanes):
    return lax.gather(
        values, lanes[..., None], LANES, (1, 1), mode=lax.GatherScatterMode.PROMISE_IN_BOUNDS
    )


ARRIVAL = (0, 1, 7, 3, 4, 2, 5, 6)


def aux_kernel(own_ref, l1_ref, l2_ref, l3_ref, l4_ref, cell_ref, out_ref):
    parts_in = [own_ref, l1_ref, l2_ref, l3_ref, l4_ref, cell_ref]
    for s in range(STRIPS):
        at = s * AUX
        for ref in parts_in:
            rows = ref.shape[0]
            out_ref[at : at + rows, :] = ref[...].astype(F32)
            at += rows


def forecast_kernel(north_ref, east_ref, mix_ref, in_ref, q_ref, t1_ref, t2_ref):
    def load(s, _):
        for r in range(ROWS):
            q_ref[pl.ds(pl.multiple_of(s * PITCH + r * LEVELS, 8), LEVELS), :] = in_ref[
                pl.ds(s * CELL_ROWS + r, LEVELS, stride=ROWS), :
            ]
        return 0

    lax.fori_loop(0, STRIPS, load, 0, unroll=4)

    def level_group(g, _):
        sub = lax.broadcasted_iota(jnp.int32, (8, COLS), 0)

        def spread(ref):
            value = jnp.full((8, COLS), ref[g * 8], F32)
            for i in range(1, 8):
                value = jnp.where(sub == i, ref[g * 8 + i], value)
            return value

        north, east, mix = spread(north_ref), spread(east_ref), spread(mix_ref)
        up, down = mix - 0.5 * north, mix + 0.5 * north
        right, left = mix - 0.5 * east, mix + 0.5 * east
        mid = -4.0 * mix

        def stage(src, dst, scale):
            a, b, c, d, e = up * scale, down * scale, right * scale, left * scale, mid * scale

            def at(ref, x):
                at_row = x // ROWS * PITCH + x % ROWS * LEVELS
                return ref.at[pl.ds(pl.multiple_of(at_row + g * 8, 8), 8), :]

            prev, cur = at(src, HEIGHT - 1)[...], at(src, 0)[...]
            first = cur
            for x in range(HEIGHT):
                nxt = first if x == HEIGHT - 1 else at(src, x + 1)[...]
                base = cur if src is q_ref else at(q_ref, x)[...]
                at(dst, x)[...] = (
                    base
                    + (a * nxt + b * prev)
                    + (c * pltpu.roll(cur, COLS - 1, 1) + d * pltpu.roll(cur, 1, 1))
                    + e * cur
                )
                prev, cur = cur, nxt

        def step(_, c):
            stage(q_ref, t1_ref, 1.0 / 3.0)
            stage(t1_ref, t2_ref, 0.5)
            stage(t2_ref, q_ref, 1.0)
            return c

        lax.fori_loop(0, STEPS, step, 0)
        return 0

    lax.fori_loop(0, LEVELS // 8, level_group, 0)

    def turn(s, _):
        q_ref[pl.ds(pl.multiple_of(FIELD + s * CELL_ROWS, 8), CELL_ROWS), :] = q_ref[
            pl.ds(pl.multiple_of(s * PITCH, 8), CELL_ROWS), :
        ].T
        return 0

    lax.fori_loop(0, STRIPS, turn, 0, unroll=4)


def select_kernel(where_ref, aux_ref, q_ref, out_ref, meta_ref, hx_ref):
    sub = lax.broadcasted_iota(jnp.int32, (COLS, 2 * COLS), 0)

    def extract(s):
        s = lax.rem(s, STRIPS)
        cell = aux_ref[pl.ds(pl.multiple_of(s * AUX + LISTS, 8), 8), :].astype(jnp.int32)
        lanes = cell & (COLS - 1)
        line = cell >> 7
        rows = (line & (ROWS - 1)) * LEVELS + (line >> 2)
        block = q_ref[pl.ds(pl.multiple_of(FIELD + s * CELL_ROWS, 8), CELL_ROWS), :]
        high = block.astype(BF16)
        rest = block - high.astype(F32)
        middle = rest.astype(BF16)
        low = (rest - middle.astype(F32)).astype(BF16)
        block = jnp.concatenate([high, middle, low], axis=1)
        found = []
        for j in range(0, OBS_CHUNKS, 2):
            row = jnp.concatenate([rows[j : j + 1], rows[j + 1 : j + 2]], axis=1)
            lane = jnp.concatenate([lanes[j : j + 1], lanes[j + 1 : j + 2]], axis=1)
            pick = jnp.where(sub == row, 1.0, 0.0).astype(BF16)
            picked = jnp.dot(
                block, jnp.concatenate([pick, pick, pick], axis=0), preferred_element_type=F32
            )
            picked = jnp.sum(jnp.where(sub == lane, picked, 0.0), axis=0, keepdims=True)
            found += [picked[:, :COLS], picked[:, COLS:]]
        for j in range(OBS_CHUNKS):
            hx_ref[pl.ds(s * OBS_CHUNKS + j, 1), :] = found[j]

    def first(i, _):
        extract(i + STRIPS - 1)
        return 0

    lax.fori_loop(0, 3, first, 0, unroll=3)

    def strip(a, _):
        for kb in range(PER_MEM):
            out_ref[pl.ds((kb * STRIPS + a) * SEND, COLS_HERE), :] = q_ref[
                pl.ds(pl.multiple_of(FIELD + a * CELL_ROWS + kb * COLS_HERE, 8), COLS_HERE), :
            ]
        sources = []
        for t in range(3):
            near = lax.rem(a + STRIPS - 1 + t, STRIPS) * OBS_CHUNKS
            for j in range(OBS_CHUNKS):
                sources.append(jnp.broadcast_to(hx_ref[pl.ds(near + j, 1), :], (8, COLS)))
        for g in range(PER_MEM // 2):
            slot = aux_ref[pl.ds(pl.multiple_of(a * AUX + g * 8, 8), 8), :].astype(jnp.int32)
            lanes = slot & (COLS - 1)
            chunk = slot >> 7
            found = lane_gather(sources[0], lanes)
            for j in range(1, META):
                found = jnp.where(chunk == j, lane_gather(sources[j], lanes), found)
            for i in range(2):
                kb = ((where_ref[1] >> 1) + ARRIVAL[g] & 7) * 2 + ((where_ref[1] & 1) ^ i)
                out_ref[pl.ds((kb * STRIPS + a) * SEND + COLS_HERE, SLOT_ROWS), :] = found[
                    i * SLOT_ROWS : (i + 1) * SLOT_ROWS
                ]
        extract(a + 2)
        return 0

    lax.fori_loop(0, STRIPS, strip, 0)

    for t in range(3):
        near = lax.rem(where_ref[0] + STRIPS - 1 + t, STRIPS)
        meta_ref[t * 8 : (t + 1) * 8, :] = aux_ref[pl.ds(pl.multiple_of(near * AUX + LISTS, 8), 8), :]


def parts(x):
    high = x.astype(BF16)
    return high, (x - high.astype(F32)).astype(BF16)


def product(a, b, dims=(((1,), (0,)), ((), ()))):
    def dot(x, y):
        return lax.dot_general(x, y, dims, preferred_element_type=F32)

    return dot(a[0], b[0]) + (dot(a[0], b[1]) + dot(a[1], b[0]))


def update_kernel(where_ref, count_ref, list_ref, cells_ref, behind_ref, here_ref, ahead_ref, in_ref, out_ref, it_ref, root_ref, meta_ref):
    members = 256
    row_id = lax.broadcasted_iota(jnp.int32, (members, members), 0)
    col_id = lax.broadcasted_iota(jnp.int32, (members, members), 1)
    diagonal = row_id == col_id
    slot_id = lax.broadcasted_iota(jnp.int32, (1, COLS), 1)

    def plus_identity(x, scale):
        return jnp.where(diagonal, x + scale, x)

    meta_ref[...] = jnp.zeros_like(meta_ref)
    for t, ref in enumerate((behind_ref, here_ref, ahead_ref)):
        meta_ref[pl.ds(t * 64, 8, stride=8), :] = cells_ref[t * 8 : (t + 1) * 8, :]
        for which in range(2):
            meta_ref[pl.ds(t * 64 + 1 + which, 8, stride=8), :] = ref[which * 8 : (which + 1) * 8, :]

    drives, scales = [], []
    for t in range(2):
        values, rhos, anomalies = [], [], []
        for h in range(2):
            slot = list_ref[pl.ds(2 * t + h, 1), :]
            wide = jnp.broadcast_to(slot, (8, COLS))
            lanes = wide & (COLS - 1)
            chunk = wide >> 7
            found = jnp.zeros((8, COLS), F32)
            for j in range(META):
                found = jnp.where(chunk == j, lane_gather(meta_ref[pl.ds(j * 8, 8), :], lanes), found)
            line = found[0:1].astype(jnp.int32)
            strip = where_ref[0] + STRIPS - 1 + (slot >> 10)
            strip = strip & (STRIPS - 1)
            place_x = (strip * ROWS + ((line >> 7) & (ROWS - 1))).astype(F32)
            place_y = (line & (COLS - 1)).astype(F32)
            centre_x = (where_ref[0] * 4).astype(F32) + 1.5
            centre_y = ((where_ref[1] * 2 + t) * 4).astype(F32) + 1.5
            dx = place_x - centre_x + 0.5 * HEIGHT
            dx = jnp.where(dx >= HEIGHT, dx - HEIGHT, dx)
            dx = jnp.where(dx < 0, dx + HEIGHT, dx) - 0.5 * HEIGHT
            dy = place_y - centre_y + 0.5 * COLS
            dy = jnp.where(dy >= COLS, dy - COLS, dy)
            dy = jnp.where(dy < 0, dy + COLS, dy) - 0.5 * COLS
            live = slot_id + h * COLS < count_ref[0, t]
            spread = found[2:3] * (1.0 + (dx * dx + dy * dy) / float(LOC * LOC))
            rho = jnp.where(live, 1.0 / spread, 0.0)
            obs = in_ref[pl.ds(COLS_HERE + 2 * t + h, members, stride=SEND), :]
            mean = jnp.sum(obs, axis=0, keepdims=True) * (1.0 / members)
            values.append(found[1:2] - mean)
            rhos.append(rho)
            anomalies.append(obs - mean)
        anomaly = jnp.concatenate(anomalies, axis=1)
        rho = jnp.concatenate(rhos, axis=1)
        innovation = jnp.concatenate(values, axis=1)
        drives.append(jnp.sum(anomaly * (rho * innovation), axis=1, keepdims=True))
        scales.append(parts(anomaly * jnp.sqrt(rho)))
    grams = [
        plus_identity(product(x, x, (((1,), (1,)), ((), ()))), (members - 1) / INFLATION) for x in scales
    ]
    norms = [
        jnp.sqrt(jnp.sum(jnp.sum(x * x, axis=0, keepdims=True), axis=1, keepdims=True)) for x in grams
    ]
    its = [gram / norm for gram, norm in zip(grams, norms)]
    factors = [plus_identity(-0.5 * it, 1.5) for it in its]
    for t in range(2):
        root_ref[t] = factors[t]
        it_ref[t] = product(parts(its[t]), parts(factors[t]))

    def iteration(_, c):
        roots = [parts(root_ref[t]) for t in range(2)]
        its = [parts(it_ref[t]) for t in range(2)]
        factors = [parts(plus_identity(-0.5 * product(roots[t], its[t]), 1.5)) for t in range(2)]
        for t in range(2):
            both = [jnp.concatenate([its[t][i], roots[t][i]], axis=0) for i in range(2)]
            both = product(both, factors[t])
            it_ref[t] = both[:members]
            root_ref[t] = both[members:]
        return c

    lax.fori_loop(0, NS_ITERS - 2, iteration, 0)

    roots = [parts(root_ref[t]) for t in range(2)]
    its = [parts(it_ref[t]) for t in range(2)]
    factors = [parts(plus_identity(-0.5 * product(roots[t], its[t]), 1.5)) for t in range(2)]
    fulls = [product(factors[t], roots[t]) for t in range(2)]
    for t in range(2):
        full = fulls[t]
        inner = jnp.sum(full * drives[t], axis=0, keepdims=True)
        shift = jnp.sum(full * inner, axis=1, keepdims=True) / norms[t]
        scale = jnp.sqrt((members - 1) / norms[t])
        root = parts(full * scale)
        for c in range(4 * t, 4 * t + 4, 2):
            x = jnp.concatenate(
                [in_ref[pl.ds(c + i, members, stride=SEND), :] for i in range(2)], axis=1
            )
            mean = jnp.sum(x, axis=0, keepdims=True) * (1.0 / members)
            x = x - mean
            moved = mean + jnp.sum(x * shift, axis=0, keepdims=True)
            out = product(root, parts(x)) + moved
            for i in range(2):
                out_ref[:, c + i] = out[:, i * COLS : (i + 1) * COLS].reshape(PER_MEM, PER_MEM, COLS)


def finish_kernel(in_ref, out_ref, turned_ref, sems):
    group = 4

    def copy(g):
        rows = pl.ds(g * group * CELL_ROWS, group * CELL_ROWS)
        return pltpu.make_async_copy(turned_ref.at[rows, :], out_ref.at[rows, :], sems.at[g])

    for g in range(PER_MEM // group):
        for m in range(g * group, (g + 1) * group):
            block = in_ref[pl.ds(m, COLS, stride=PER_MEM), :].T
            for r in range(ROWS):
                turned_ref[pl.ds(m * CELL_ROWS + r, LEVELS, stride=ROWS), :] = block[
                    r * LEVELS : (r + 1) * LEVELS
                ]
        copy(g).start()
    for g in range(PER_MEM // group):
        copy(g).wait()


PARAMS = pltpu.CompilerParams(vmem_limit_bytes=20 * 1024 * 1024)
SMEM = pl.BlockSpec(memory_space=pltpu.SMEM)
VMEM = pl.BlockSpec(memory_space=pltpu.VMEM)


def shards(prior, north, east, mix, obs_cell, obs_value, obs_var, tile_list, tile_count):
    dom, mem = lax.axis_index("dom"), lax.axis_index("mem")
    where = jnp.stack([dom, mem]).astype(jnp.int32)
    own = tile_list.reshape(SLOT_ROWS, COLS)
    def shifted(x, by):
        return lax.ppermute(x, "mem", [((i + by) % PER_MEM, i) for i in range(PER_MEM)])

    chip = jnp.concatenate(
        [own, lax.ppermute(own, "mem", [(i, i ^ 1) for i in range(PER_MEM)])], axis=0
    )
    ahead, behind = shifted(chip, 2), shifted(chip, -2)
    pieces = [
        chip, ahead, behind,
        shifted(jnp.concatenate([chip, ahead, behind], axis=0), 6),
        shifted(jnp.concatenate([chip, ahead], axis=0), -6),
    ]
    whole = lax.all_to_all(
        prior.reshape(PER_MEM, CELL_ROWS, COLS), "dom", split_axis=0, concat_axis=0, tiled=True
    )
    observed = jnp.concatenate([obs_value, obs_var]).reshape(2 * OBS_CHUNKS, COLS)
    observed, whole = lax.optimization_barrier((observed, whole))
    ring = [(i, (i + 1) % STRIPS) for i in range(STRIPS)]
    behind_obs = lax.ppermute(observed, "dom", ring)
    ahead_obs = lax.ppermute(observed, "dom", [(b, a) for a, b in ring])
    aux = pl.pallas_call(
        aux_kernel,
        compiler_params=PARAMS,
        name="aux",
        out_shape=jax.ShapeDtypeStruct((STRIPS * AUX, COLS), F32),
        in_specs=[VMEM] * 6,
        out_specs=VMEM,
    )(
        *pieces,
        obs_cell.reshape(OBS_CHUNKS, COLS),
    )
    every = lax.all_to_all(
        aux.reshape(STRIPS, AUX, COLS), "dom", split_axis=0, concat_axis=0, tiled=True
    )
    levels = pl.pallas_call(
        forecast_kernel,
        compiler_params=PARAMS,
        cost_estimate=pl.CostEstimate(flops=30_000_000, bytes_accessed=60_000_000, transcendentals=0),
        name="forecast",
        out_shape=jax.ShapeDtypeStruct((FIELD + STRIPS * CELL_ROWS, COLS), F32),
        in_specs=[SMEM, SMEM, SMEM, VMEM],
        out_specs=VMEM,
        scratch_shapes=[pltpu.VMEM((STRIPS * PITCH, COLS), F32)] * 2,
    )(north, east, mix, whole.reshape(STRIPS * CELL_ROWS, COLS))
    sent, near = pl.pallas_call(
        select_kernel,
        compiler_params=PARAMS,
        name="select",
        out_shape=(
            jax.ShapeDtypeStruct((PER_MEM * STRIPS * SEND, COLS), F32),
            jax.ShapeDtypeStruct((META, COLS), F32),
        ),
        in_specs=[SMEM, VMEM, VMEM],
        out_specs=(VMEM, VMEM),
        scratch_shapes=[pltpu.VMEM((STRIPS * OBS_CHUNKS, COLS), F32)],
    )(where, every.reshape(STRIPS * AUX, COLS), levels)
    tiles = lax.all_to_all(
        sent.reshape(PER_MEM * STRIPS, SEND // 4, 4, COLS),
        ("mem", "dom"), split_axis=0, concat_axis=0, tiled=True,
    )
    updated = pl.pallas_call(
        update_kernel,
        compiler_params=PARAMS,
        name="update",
        out_shape=jax.ShapeDtypeStruct((PER_MEM, COLS_HERE, PER_MEM, COLS), F32),
        in_specs=[SMEM, SMEM] + [VMEM] * 6,
        out_specs=VMEM,
        scratch_shapes=[
            pltpu.VMEM((2, 256, 256), F32),
            pltpu.VMEM((2, 256, 256), F32),
            pltpu.VMEM((META * 8, COLS), F32),
        ],
    )(where, tile_count, own, near, behind_obs, observed, ahead_obs, tiles.reshape(PER_MEM * STRIPS * SEND, COLS))
    back = lax.all_to_all(
        updated.reshape(PER_MEM, COLS_HERE * PER_MEM, COLS), "mem", split_axis=0, concat_axis=0, tiled=True
    )
    result = pl.pallas_call(
        finish_kernel,
        compiler_params=PARAMS,
        name="finish",
        out_shape=jax.ShapeDtypeStruct((PER_MEM * CELL_ROWS, COLS), F32),
        in_specs=[VMEM],
        out_specs=pl.BlockSpec(memory_space=pl.ANY),
        scratch_shapes=[
            pltpu.VMEM((PER_MEM * CELL_ROWS, COLS), F32),
            pltpu.SemaphoreType.DMA((4,)),
        ],
    )(back.reshape(PER_MEM * COLS_HERE * PER_MEM, COLS))
    return result.reshape(PER_MEM, LEVELS, ROWS, COLS)


def solution(mesh):
    placed = (
        P("mem", None, "dom", None),
        P(),
        P(),
        P(),
        P("dom"),
        P("dom"),
        P("dom"),
        P("dom", "mem", None),
        P("dom", "mem"),
    )
    return jax.shard_map(
        shards, mesh=mesh, in_specs=placed, out_specs=P("mem", None, "dom", None), check_vma=False
    )
```

```python
import jax
import jax.numpy as jnp
from jax import lax
from jax.experimental import pallas as pl
from jax.experimental.pallas import tpu as pltpu
from jax.sharding import PartitionSpec as P

LOC = 8
STEPS = 3
NS_ITERS = 5
INFLATION = 1.1

F32 = jnp.float32
BF16 = jnp.bfloat16
LEVELS = 32
ROWS = 4
COLS = 128
CELL_ROWS = LEVELS * ROWS
OBS_CHUNKS = 8
META = 3 * OBS_CHUNKS
SLOT_ROWS = 4
COLS_HERE = 8
SEND = COLS_HERE + SLOT_ROWS
PER_MEM = 16
STRIPS = 16
HEIGHT = STRIPS * ROWS
PITCH = CELL_ROWS + 8
FIELD = STRIPS * PITCH
LISTS = PER_MEM * SLOT_ROWS
AUX = LISTS + OBS_CHUNKS


LANES = lax.GatherDimensionNumbers(
    offset_dims=(),
    collapsed_slice_dims=(1,),
    start_index_map=(1,),
    operand_batching_dims=(0,),
    start_indices_batching_dims=(0,),
)


def lane_gather(values, lanes):
    return lax.gather(
        values, lanes[..., None], LANES, (1, 1), mode=lax.GatherScatterMode.PROMISE_IN_BOUNDS
    )


ARRIVAL = (0, 1, 7, 3, 4, 2, 5, 6)


def aux_kernel(own_ref, l1_ref, l2_ref, l3_ref, l4_ref, cell_ref, out_ref):
    parts_in = [own_ref, l1_ref, l2_ref, l3_ref, l4_ref, cell_ref]
    for s in range(STRIPS):
        at = s * AUX
        for ref in parts_in:
            rows = ref.shape[0]
            out_ref[at : at + rows, :] = ref[...].astype(F32)
            at += rows


def forecast_kernel(north_ref, east_ref, mix_ref, in_ref, q_ref, t1_ref, t2_ref):
    def load(s, _):
        for r in range(ROWS):
            q_ref[pl.ds(pl.multiple_of(s * PITCH + r * LEVELS, 8), LEVELS), :] = in_ref[
                pl.ds(s * CELL_ROWS + r, LEVELS, stride=ROWS), :
            ]
        return 0

    lax.fori_loop(0, STRIPS, load, 0, unroll=4)

    def level_group(g, _):
        sub = lax.broadcasted_iota(jnp.int32, (8, COLS), 0)

        def spread(ref):
            value = jnp.full((8, COLS), ref[g * 8], F32)
            for i in range(1, 8):
                value = jnp.where(sub == i, ref[g * 8 + i], value)
            return value

        north, east, mix = spread(north_ref), spread(east_ref), spread(mix_ref)
        up, down = mix - 0.5 * north, mix + 0.5 * north
        right, left = mix - 0.5 * east, mix + 0.5 * east
        mid = -4.0 * mix

        def stage(src, dst, scale):
            a, b, c, d, e = up * scale, down * scale, right * scale, left * scale, mid * scale

            def at(ref, x):
                at_row = x // ROWS * PITCH + x % ROWS * LEVELS
                return ref.at[pl.ds(pl.multiple_of(at_row + g * 8, 8), 8), :]

            prev, cur = at(src, HEIGHT - 1)[...], at(src, 0)[...]
            first = cur
            for x in range(HEIGHT):
                nxt = first if x == HEIGHT - 1 else at(src, x + 1)[...]
                base = cur if src is q_ref else at(q_ref, x)[...]
                at(dst, x)[...] = (
                    base
                    + (a * nxt + b * prev)
                    + (c * pltpu.roll(cur, COLS - 1, 1) + d * pltpu.roll(cur, 1, 1))
                    + e * cur
                )
                prev, cur = cur, nxt

        def step(_, c):
            stage(q_ref, t1_ref, 1.0 / 3.0)
            stage(t1_ref, t2_ref, 0.5)
            stage(t2_ref, q_ref, 1.0)
            return c

        lax.fori_loop(0, STEPS, step, 0)
        return 0

    lax.fori_loop(0, LEVELS // 8, level_group, 0)

    def turn(s, _):
        q_ref[pl.ds(pl.multiple_of(FIELD + s * CELL_ROWS, 8), CELL_ROWS), :] = q_ref[
            pl.ds(pl.multiple_of(s * PITCH, 8), CELL_ROWS), :
        ].T
        return 0

    lax.fori_loop(0, STRIPS, turn, 0, unroll=4)


def select_kernel(where_ref, aux_ref, q_ref, behind_ref, ahead_ref, out_ref, meta_ref, hx_ref):
    sub = lax.broadcasted_iota(jnp.int32, (COLS, 2 * COLS), 0)

    def extract(s):
        s = lax.rem(s, STRIPS)
        cell = aux_ref[pl.ds(pl.multiple_of(s * AUX + LISTS, 8), 8), :].astype(jnp.int32)
        lanes = cell & (COLS - 1)
        line = cell >> 7
        rows = (line & (ROWS - 1)) * LEVELS + (line >> 2)
        block = q_ref[pl.ds(pl.multiple_of(FIELD + s * CELL_ROWS, 8), CELL_ROWS), :]
        high = block.astype(BF16)
        rest = block - high.astype(F32)
        middle = rest.astype(BF16)
        low = (rest - middle.astype(F32)).astype(BF16)
        block = jnp.concatenate([high, middle, low], axis=1)
        found = []
        for j in range(0, OBS_CHUNKS, 2):
            row = jnp.concatenate([rows[j : j + 1], rows[j + 1 : j + 2]], axis=1)
            lane = jnp.concatenate([lanes[j : j + 1], lanes[j + 1 : j + 2]], axis=1)
            pick = jnp.where(sub == row, 1.0, 0.0).astype(BF16)
            picked = jnp.dot(
                block, jnp.concatenate([pick, pick, pick], axis=0), preferred_element_type=F32
            )
            picked = jnp.sum(jnp.where(sub == lane, picked, 0.0), axis=0, keepdims=True)
            found += [picked[:, :COLS], picked[:, COLS:]]
        for j in range(OBS_CHUNKS):
            hx_ref[pl.ds(s * OBS_CHUNKS + j, 1), :] = found[j]

    def first(i, _):
        extract(i + STRIPS - 1)
        return 0

    lax.fori_loop(0, 3, first, 0, unroll=3)

    def strip(a, _):
        for kb in range(PER_MEM):
            out_ref[pl.ds((kb * STRIPS + a) * SEND, COLS_HERE), :] = q_ref[
                pl.ds(pl.multiple_of(FIELD + a * CELL_ROWS + kb * COLS_HERE, 8), COLS_HERE), :
            ]
        sources = []
        for t in range(3):
            near = lax.rem(a + STRIPS - 1 + t, STRIPS) * OBS_CHUNKS
            for j in range(OBS_CHUNKS):
                sources.append(jnp.broadcast_to(hx_ref[pl.ds(near + j, 1), :], (8, COLS)))
        for g in range(PER_MEM // 2):
            slot = aux_ref[pl.ds(pl.multiple_of(a * AUX + g * 8, 8), 8), :].astype(jnp.int32)
            lanes = slot & (COLS - 1)
            chunk = slot >> 7
            found = lane_gather(sources[0], lanes)
            for j in range(1, META):
                found = jnp.where(chunk == j, lane_gather(sources[j], lanes), found)
            for i in range(2):
                kb = ((where_ref[1] >> 1) + ARRIVAL[g] & 7) * 2 + ((where_ref[1] & 1) ^ i)
                out_ref[pl.ds((kb * STRIPS + a) * SEND + COLS_HERE, SLOT_ROWS), :] = found[
                    i * SLOT_ROWS : (i + 1) * SLOT_ROWS
                ]
        extract(a + 2)
        return 0

    lax.fori_loop(0, STRIPS, strip, 0)

    for t in range(3):
        near = lax.rem(where_ref[0] + STRIPS - 1 + t, STRIPS)
        meta_ref[t * 8 : (t + 1) * 8, :] = aux_ref[pl.ds(pl.multiple_of(near * AUX + LISTS, 8), 8), :]


def parts(x):
    high = x.astype(BF16)
    return high, (x - high.astype(F32)).astype(BF16)


def product(a, b, dims=(((1,), (0,)), ((), ()))):
    def dot(x, y):
        return lax.dot_general(x, y, dims, preferred_element_type=F32)

    return dot(a[0], b[0]) + (dot(a[0], b[1]) + dot(a[1], b[0]))


def update_kernel(where_ref, count_ref, list_ref, cells_ref, behind_ref, here_ref, ahead_ref, in_ref, out_ref, it_ref, root_ref, meta_ref):
    members = 256
    row_id = lax.broadcasted_iota(jnp.int32, (members, members), 0)
    col_id = lax.broadcasted_iota(jnp.int32, (members, members), 1)
    diagonal = row_id == col_id
    slot_id = lax.broadcasted_iota(jnp.int32, (1, COLS), 1)

    def plus_identity(x, scale):
        return jnp.where(diagonal, x + scale, x)

    meta_ref[...] = jnp.zeros_like(meta_ref)
    for t, ref in enumerate((behind_ref, here_ref, ahead_ref)):
        meta_ref[pl.ds(t * 64, 8, stride=8), :] = cells_ref[t * 8 : (t + 1) * 8, :]
        for which in range(2):
            meta_ref[pl.ds(t * 64 + 1 + which, 8, stride=8), :] = ref[which * 8 : (which + 1) * 8, :]

    drives, scales = [], []
    for t in range(2):
        values, rhos, anomalies = [], [], []
        for h in range(2):
            slot = list_ref[pl.ds(2 * t + h, 1), :]
            wide = jnp.broadcast_to(slot, (8, COLS))
            lanes = wide & (COLS - 1)
            chunk = wide >> 7
            found = jnp.zeros((8, COLS), F32)
            for j in range(META):
                found = jnp.where(chunk == j, lane_gather(meta_ref[pl.ds(j * 8, 8), :], lanes), found)
            line = found[0:1].astype(jnp.int32)
            strip = where_ref[0] + STRIPS - 1 + (slot >> 10)
            strip = strip & (STRIPS - 1)
            place_x = (strip * ROWS + ((line >> 7) & (ROWS - 1))).astype(F32)
            place_y = (line & (COLS - 1)).astype(F32)
            centre_x = (where_ref[0] * 4).astype(F32) + 1.5
            centre_y = ((where_ref[1] * 2 + t) * 4).astype(F32) + 1.5
            dx = place_x - centre_x + 0.5 * HEIGHT
            dx = jnp.where(dx >= HEIGHT, dx - HEIGHT, dx)
            dx = jnp.where(dx < 0, dx + HEIGHT, dx) - 0.5 * HEIGHT
            dy = place_y - centre_y + 0.5 * COLS
            dy = jnp.where(dy >= COLS, dy - COLS, dy)
            dy = jnp.where(dy < 0, dy + COLS, dy) - 0.5 * COLS
            live = slot_id + h * COLS < count_ref[0, t]
            spread = found[2:3] * (1.0 + (dx * dx + dy * dy) / float(LOC * LOC))
            rho = jnp.where(live, 1.0 / spread, 0.0)
            obs = in_ref[pl.ds(COLS_HERE + 2 * t + h, members, stride=SEND), :]
            mean = jnp.sum(obs, axis=0, keepdims=True) * (1.0 / members)
            values.append(found[1:2] - mean)
            rhos.append(rho)
            anomalies.append(obs - mean)
        anomaly = jnp.concatenate(anomalies, axis=1)
        rho = jnp.concatenate(rhos, axis=1)
        innovation = jnp.concatenate(values, axis=1)
        drives.append(jnp.sum(anomaly * (rho * innovation), axis=1, keepdims=True))
        scales.append(parts(anomaly * jnp.sqrt(rho)))
    grams = [
        plus_identity(product(x, x, (((1,), (1,)), ((), ()))), (members - 1) / INFLATION) for x in scales
    ]
    norms = [
        jnp.sqrt(jnp.sum(jnp.sum(x * x, axis=0, keepdims=True), axis=1, keepdims=True)) for x in grams
    ]
    its = [gram / norm for gram, norm in zip(grams, norms)]
    factors = [plus_identity(-0.5 * it, 1.5) for it in its]
    for t in range(2):
        root_ref[t] = factors[t]
        it_ref[t] = product(parts(its[t]), parts(factors[t]))

    def iteration(_, c):
        roots = [parts(root_ref[t]) for t in range(2)]
        its = [parts(it_ref[t]) for t in range(2)]
        factors = [parts(plus_identity(-0.5 * product(roots[t], its[t]), 1.5)) for t in range(2)]
        for t in range(2):
            both = [jnp.concatenate([its[t][i], roots[t][i]], axis=0) for i in range(2)]
            both = product(both, factors[t])
            it_ref[t] = both[:members]
            root_ref[t] = both[members:]
        return c

    lax.fori_loop(0, NS_ITERS - 2, iteration, 0)

    roots = [parts(root_ref[t]) for t in range(2)]
    its = [parts(it_ref[t]) for t in range(2)]
    factors = [parts(plus_identity(-0.5 * product(roots[t], its[t]), 1.5)) for t in range(2)]
    fulls = [product(factors[t], roots[t]) for t in range(2)]
    for t in range(2):
        full = fulls[t]
        inner = jnp.sum(full * drives[t], axis=0, keepdims=True)
        shift = jnp.sum(full * inner, axis=1, keepdims=True) / norms[t]
        scale = jnp.sqrt((members - 1) / norms[t])
        root = parts(full * scale)
        for c in range(4 * t, 4 * t + 4, 2):
            x = jnp.concatenate(
                [in_ref[pl.ds(c + i, members, stride=SEND), :] for i in range(2)], axis=1
            )
            mean = jnp.sum(x, axis=0, keepdims=True) * (1.0 / members)
            x = x - mean
            moved = mean + jnp.sum(x * shift, axis=0, keepdims=True)
            out = product(root, parts(x)) + moved
            for i in range(2):
                out_ref[:, c + i] = out[:, i * COLS : (i + 1) * COLS].reshape(PER_MEM, PER_MEM, COLS)


def finish_kernel(in_ref, out_ref, turned_ref, sems):
    group = 4

    def copy(g):
        rows = pl.ds(g * group * CELL_ROWS, group * CELL_ROWS)
        return pltpu.make_async_copy(turned_ref.at[rows, :], out_ref.at[rows, :], sems.at[g])

    for g in range(PER_MEM // group):
        for m in range(g * group, (g + 1) * group):
            block = in_ref[pl.ds(m, COLS, stride=PER_MEM), :].T
            for r in range(ROWS):
                turned_ref[pl.ds(m * CELL_ROWS + r, LEVELS, stride=ROWS), :] = block[
                    r * LEVELS : (r + 1) * LEVELS
                ]
        copy(g).start()
    for g in range(PER_MEM // group):
        copy(g).wait()


PARAMS = pltpu.CompilerParams(vmem_limit_bytes=20 * 1024 * 1024)
SMEM = pl.BlockSpec(memory_space=pltpu.SMEM)
VMEM = pl.BlockSpec(memory_space=pltpu.VMEM)


def shards(prior, north, east, mix, obs_cell, obs_value, obs_var, tile_list, tile_count):
    dom, mem = lax.axis_index("dom"), lax.axis_index("mem")
    where = jnp.stack([dom, mem]).astype(jnp.int32)
    own = tile_list.reshape(SLOT_ROWS, COLS)
    def shifted(x, by):
        return lax.ppermute(x, "mem", [((i + by) % PER_MEM, i) for i in range(PER_MEM)])

    chip = jnp.concatenate(
        [own, lax.ppermute(own, "mem", [(i, i ^ 1) for i in range(PER_MEM)])], axis=0
    )
    ahead, behind = shifted(chip, 2), shifted(chip, -2)
    pieces = [
        chip, ahead, behind,
        shifted(jnp.concatenate([chip, ahead, behind], axis=0), 6),
        shifted(jnp.concatenate([chip, ahead], axis=0), -6),
    ]
    whole = lax.all_to_all(
        prior.reshape(PER_MEM, CELL_ROWS, COLS), "dom", split_axis=0, concat_axis=0, tiled=True
    )
    observed = jnp.concatenate([obs_value, obs_var]).reshape(2 * OBS_CHUNKS, COLS)
    observed, whole = lax.optimization_barrier((observed, whole))
    ring = [(i, (i + 1) % STRIPS) for i in range(STRIPS)]
    behind_obs = lax.ppermute(observed, "dom", ring)
    ahead_obs = lax.ppermute(observed, "dom", [(b, a) for a, b in ring])
    aux = pl.pallas_call(
        aux_kernel,
        compiler_params=PARAMS,
        name="aux",
        out_shape=jax.ShapeDtypeStruct((STRIPS * AUX, COLS), F32),
        in_specs=[VMEM] * 6,
        out_specs=VMEM,
    )(
        *pieces,
        obs_cell.reshape(OBS_CHUNKS, COLS),
    )
    every = lax.all_to_all(
        aux.reshape(STRIPS, AUX, COLS), "dom", split_axis=0, concat_axis=0, tiled=True
    )
    levels = pl.pallas_call(
        forecast_kernel,
        compiler_params=PARAMS,
        cost_estimate=pl.CostEstimate(flops=30_000_000, bytes_accessed=60_000_000, transcendentals=0),
        name="forecast",
        out_shape=jax.ShapeDtypeStruct((FIELD + STRIPS * CELL_ROWS, COLS), F32),
        in_specs=[SMEM, SMEM, SMEM, VMEM],
        out_specs=VMEM,
        scratch_shapes=[pltpu.VMEM((STRIPS * PITCH, COLS), F32)] * 2,
    )(north, east, mix, whole.reshape(STRIPS * CELL_ROWS, COLS))
    sent, near = pl.pallas_call(
        select_kernel,
        compiler_params=PARAMS,
        name="select",
        out_shape=(
            jax.ShapeDtypeStruct((PER_MEM * STRIPS * SEND, COLS), F32),
            jax.ShapeDtypeStruct((META, COLS), F32),
        ),
        in_specs=[SMEM, VMEM, VMEM] + [pl.BlockSpec(memory_space=pl.ANY)] * 2,
        out_specs=(VMEM, VMEM),
        scratch_shapes=[pltpu.VMEM((STRIPS * OBS_CHUNKS, COLS), F32)],
    )(where, every.reshape(STRIPS * AUX, COLS), levels, behind_obs, ahead_obs)
    tiles = lax.all_to_all(
        sent.reshape(PER_MEM * STRIPS, SEND // 4, 4, COLS),
        ("mem", "dom"), split_axis=0, concat_axis=0, tiled=True,
    )
    updated = pl.pallas_call(
        update_kernel,
        compiler_params=PARAMS,
        name="update",
        out_shape=jax.ShapeDtypeStruct((PER_MEM, COLS_HERE, PER_MEM, COLS), F32),
        in_specs=[SMEM, SMEM] + [VMEM] * 6,
        out_specs=VMEM,
        scratch_shapes=[
            pltpu.VMEM((2, 256, 256), F32),
            pltpu.VMEM((2, 256, 256), F32),
            pltpu.VMEM((META * 8, COLS), F32),
        ],
    )(where, tile_count, own, near, behind_obs, observed, ahead_obs, tiles.reshape(PER_MEM * STRIPS * SEND, COLS))
    back = lax.all_to_all(
        updated.reshape(PER_MEM, COLS_HERE * PER_MEM, COLS), "mem", split_axis=0, concat_axis=0, tiled=True
    )
    result = pl.pallas_call(
        finish_kernel,
        compiler_params=PARAMS,
        name="finish",
        out_shape=jax.ShapeDtypeStruct((PER_MEM * CELL_ROWS, COLS), F32),
        in_specs=[VMEM],
        out_specs=pl.BlockSpec(memory_space=pl.ANY),
        scratch_shapes=[
            pltpu.VMEM((PER_MEM * CELL_ROWS, COLS), F32),
            pltpu.SemaphoreType.DMA((4,)),
        ],
    )(back.reshape(PER_MEM * COLS_HERE * PER_MEM, COLS))
    return result.reshape(PER_MEM, LEVELS, ROWS, COLS)


def solution(mesh):
    placed = (
        P("mem", None, "dom", None),
        P(),
        P(),
        P(),
        P("dom"),
        P("dom"),
        P("dom"),
        P("dom", "mem", None),
        P("dom", "mem"),
    )
    return jax.shard_map(
        shards, mesh=mesh, in_specs=placed, out_specs=P("mem", None, "dom", None), check_vma=False
    )
```
